32 devices in a mesh: dom: 8 (over z, x), rep: 4 (over y, core).
Axes of the slice: x: 2, y: 2, z: 4, core: 2. Of those that a mesh axis runs over, the one named last changes fastest.
Arguments:
- elem_rows: bfloat16 [65536, 512], P(('dom', 'rep')), may hold values from -6 to 6
- elem_block: int32 [65536], P(('dom', 'rep')), may hold values from 0 to 3
- send_lists: int32 [65536], P(('dom', 'rep')), may hold values from 0 to 2047, as said below
- halo_block: int32 [65536], P(('dom', 'rep')), may hold values from 0 to 3
- born_rows: bfloat16 [2048, 512], P(('dom', 'rep')), may hold values from -6 to 6
- born_owner: int32 [2048, 1], P(('dom', 'rep')), may hold values from 0 to 31; in each aligned block of 64 rows (0 to 63, 64 to 127, ...) at most 4 rows name the same one
- mass: float32 [16384], P(('dom', 'rep')), may hold values from 0.5 to 4
Outputs:
- factor: float32 [16384, 512], P(('dom', 'rep'))
The draws below stay inside these ranges and needn't reach their ends.
Inputs may be any that keep to these rules, and one draw needn't show every extreme that they name: `send_lists`: each half of one device's list names 1024 distinct rows of that device. `born_owner`: among the born rows of one device at most 4 name the same owner.
All inputs are finite; a program needn't handle non-finite values.
Results may differ from the reference program's by a relative error of at most 0.0003.
Values may be sent and summed in bfloat16 or wider, within the bound.
A program may use at most 64 MiB of HBM per device.

```python
import math
import jax
import jax.numpy as jnp
import numpy as np
from jax import lax

W = 512
E_DEV = 2048
H = 1024
CAP = 4
NBLK = 32
BORN_DEV = 64
N_DOM = 8
N_REP = 4


def draw_send_lists(key, part):
    device_keys = jax.random.split(jax.random.fold_in(key, 17), NBLK * 2)

    def one_half(half_key):
        return jax.random.permutation(half_key, E_DEV)[:H]
    chosen = jax.vmap(one_half)(device_keys)
    return chosen.reshape(-1).astype(jnp.int32)


def touch_ends(values, key, smallest, high):
    longest = values.shape.index(max(values.shape))
    spots = []
    for shift in (0, 1):
        where = [jax.random.randint(jax.random.fold_in(key, axis), (), 0, length) for axis, length in enumerate(values.shape)]
        where[longest] = (where[longest] + shift) % values.shape[longest]
        spots.append(tuple(where))
    return values.at[spots[0]].set(smallest).at[spots[1]].set(high)


def block_scale(key, dims, cuts, low, top_value):
    level = 1.0
    for dim, blocks in cuts:
        heights = jax.random.uniform(jax.random.fold_in(jax.random.fold_in(key, 6), dim), (blocks,), jnp.float32, low / len(cuts), top_value / len(cuts))
        level = level * jnp.repeat(jnp.exp(heights), dims[dim] // blocks).reshape((-1,) + (1,) * (len(dims) - 1 - dim))
    return level


def assign_block(key, own, number, rows, amount, top, bound, skew):
    ranking = jax.random.permutation(key, amount)
    packed, common = portions_of(amount, rows * top, bound, skew, True), portions_of(amount, rows * top, bound, skew, False)
    places = jnp.arange(amount)

    def named(tallies, offset_by):
        used = int((tallies > 0).sum())
        fixed = max(1, used // 4)
        passed = fixed + (places - fixed + offset_by * (used - fixed)) % max(1, amount - fixed)
        return jnp.zeros((amount,), jnp.int32).at[ranking[jnp.where(places < fixed, places, passed)]].set(jnp.asarray(tallies, jnp.int32))

    tallies = jnp.where(number % 4 == 0, named(packed, number // 4), named(common, number - number // 4 - 1))
    mixed = jax.random.permutation(jax.random.fold_in(own, 3), amount)
    donor, taker = mixed[0:amount // 2 * 2:2], mixed[1:amount // 2 * 2:2]
    room = jnp.minimum(tallies[donor] - 1, bound - tallies[taker]) // 2
    room = jnp.where((donor == ranking[0]) | (taker == ranking[0]) | (tallies[taker] == 0), 0, jnp.maximum(room, 0))
    passed = jax.random.randint(jax.random.fold_in(own, 4), (amount // 2,), 0, 1 << 20) % (room + 1)
    tallies = tallies.at[donor].add(-passed).at[taker].add(passed)
    members = jnp.searchsorted(jnp.cumsum(tallies), jnp.arange(rows * top), side="right").astype(jnp.int32)
    table = members.reshape(top, rows).T
    table = table[jax.random.permutation(jax.random.fold_in(own, 1), rows)]
    offset_by = jax.random.randint(jax.random.fold_in(own, 2), (rows, 1), 0, top)
    return jnp.take_along_axis(table, (jnp.arange(top)[None, :] + offset_by) % top, axis=1)


def portions_of(number_of, total, bound, slope, full):
    weights = [(1 << 20) // math.isqrt(rank ** slope) + 1 for rank in range(1, number_of + 1)]
    largest = bound if full else min(bound, max(-(-total // number_of), total * weights[0] // sum(weights)))
    least = 1 if total - largest >= number_of - 1 else 0
    holding, spare = [largest] + [least] * (number_of - 1), total - largest - least * (number_of - 1)
    while spare > 0:
        free = [i for i in range(1, number_of) if holding[i] < largest] or [i for i in range(1, number_of) if holding[i] < bound]
        pool, left = sum([weights[i] for i in free]), spare
        for i in free:
            extra = min(bound - holding[i], max(1, left * weights[i] // pool), spare)
            holding[i] = holding[i] + extra
            spare = spare - extra
    return np.array(holding)


def normal_values(key, shape, deviation, limit, cuts=(), held_as=jnp.bfloat16):
    result = jax.random.normal(key, shape, jnp.float32) * deviation
    if len(cuts) > 0:
        result = block_scale(key, shape, cuts, -0.22, 0.18) * result
    return jnp.clip(result, min=-limit, max=limit).astype(held_as)


def setup_inputs(seed: int = 0) -> dict:
    streams_of = jax.random.split(jax.random.key(seed), 8)
    elem_rows = normal_values(streams_of[0], (NBLK * E_DEV, W), 1.0, 6.0, ((0, 32),))
    elem_block = touch_ends(jax.random.randint(streams_of[1], (NBLK * E_DEV,), 0, N_REP), jax.random.fold_in(streams_of[1], 1), 0, N_REP - 1).astype(jnp.int32)
    send_lists = draw_send_lists(jax.random.fold_in(streams_of[7], 71), 0)
    halo_block = touch_ends(jax.random.randint(streams_of[3], (NBLK * 2 * H,), 0, N_REP), jax.random.fold_in(streams_of[3], 1), 0, N_REP - 1).astype(jnp.int32)
    born_rows = normal_values(streams_of[4], (NBLK * BORN_DEV, W), 1.0, 6.0, ((0, 32),))
    born_owner_keys = jax.random.split(jax.random.fold_in(streams_of[5], 1), (NBLK * BORN_DEV) // BORN_DEV)
    born_owner_turns = jax.random.permutation(jax.random.fold_in(streams_of[5], 3), (NBLK * BORN_DEV) // BORN_DEV)
    born_owner = jax.vmap(lambda own, number: assign_block(jax.random.fold_in(streams_of[5], 2), own, number, BORN_DEV, NBLK, 1, CAP, 2))(born_owner_keys, born_owner_turns).reshape((NBLK * BORN_DEV, 1))
    mass = jnp.clip(0.5 + 3.5 * jax.random.uniform(streams_of[6], (NBLK * W,), jnp.float32) ** block_scale(streams_of[6], (NBLK * W,), ((0, 32),), -0.2, 0.2), 0.5, 4.0)
    return {"elem_rows": elem_rows, "elem_block": elem_block, "send_lists": send_lists, "halo_block": halo_block, "born_rows": born_rows, "born_owner": born_owner, "mass": mass}


def pick_rows(row_data, chosen):
    return jnp.take(row_data, chosen, axis=0)

def reference(elem_rows, elem_block, send_lists, halo_block, born_rows, born_owner, mass):
    rows_dev = elem_rows.reshape(NBLK, E_DEV, W)
    list_pairs = send_lists.reshape(NBLK, 2 * H)
    listed_rows = jax.vmap(pick_rows)(rows_dev, list_pairs).reshape(N_DOM, N_REP, 2, H, W)
    to_lower = listed_rows[:, :, 0]
    to_upper = listed_rows[:, :, 1]
    empty_part = jnp.zeros((1, N_REP, H, W), jnp.bfloat16)
    from_lower = jnp.concatenate([empty_part, to_upper[:-1]], axis=0)
    from_upper = jnp.concatenate([to_lower[1:], empty_part], axis=0)
    halo_rows = jnp.concatenate([from_lower, from_upper], axis=2).reshape(N_DOM, N_REP * 2 * H, W)
    halo_ids = halo_block.reshape(N_DOM, N_REP * 2 * H)
    own_rows = elem_rows.reshape(N_DOM, N_REP * E_DEV, W)
    own_ids = elem_block.reshape(N_DOM, N_REP * E_DEV)
    row_pool = jnp.concatenate([own_rows, halo_rows], axis=1)
    pool_ids = jnp.concatenate([own_ids, halo_ids], axis=1)
    owner_codes = born_owner[:, 0]
    sorted_order = jnp.argsort(owner_codes, stable=True)
    window = NBLK * CAP
    sorted_rows = jnp.concatenate([born_rows[sorted_order], jnp.zeros((window, W), jnp.bfloat16)], axis=0)
    owner_counts = jax.ops.segment_sum(jnp.ones_like(owner_codes), owner_codes, NBLK).astype(jnp.int32)
    offsets = (jnp.cumsum(owner_counts) - owner_counts).astype(jnp.int32)
    mass_blocks = mass.reshape(NBLK, W)

    def factor_block(block_index):
        partition = block_index // N_REP
        block_id = block_index % N_REP
        row_data = row_pool[partition]
        in_block = pool_ids[partition] == block_id
        masked = jnp.where(in_block[:, None], row_data, jnp.zeros((), jnp.bfloat16))
        block_gram = jnp.dot(masked.T.astype(jnp.float32), row_data.astype(jnp.float32), preferred_element_type=jnp.float32)
        window_rows = lax.dynamic_slice_in_dim(sorted_rows, offsets[block_index].astype(jnp.int32), window, 0)
        live_rows = jnp.arange(window, dtype=jnp.int32) < owner_counts[block_index]
        born_masked = jnp.where(live_rows[:, None], window_rows, jnp.zeros((), jnp.bfloat16))
        block_gram = block_gram + jnp.dot(born_masked.T.astype(jnp.float32), window_rows.astype(jnp.float32), preferred_element_type=jnp.float32)
        system = jnp.diag(mass_blocks[block_index]) + block_gram / W
        return jnp.linalg.cholesky(system)
    factors = lax.map(factor_block, jnp.arange(NBLK, dtype=jnp.int32))
    return factors.reshape(NBLK * W, W)
```

```python
import functools

import jax
import jax.numpy as jnp
from jax import lax
from jax.experimental import pallas as pl
from jax.experimental.pallas import tpu as pltpu
from jax.sharding import PartitionSpec as P

CAP = 4
F=jnp.float32; BF=jnp.bfloat16

def split3(v):
    hi=v.astype(BF); r=v-hi.astype(F); mid=r.astype(BF); lo=(r-mid.astype(F)).astype(BF)
    return hi,mid,lo

def chol_diag(D, A):
    nb=D.shape[0]; st=16
    r_i=lax.broadcasted_iota(jnp.int32,(nb,nb),0); c_i=lax.broadcasted_iota(jnp.int32,(nb,nb),1)
    A[:, :nb]=D
    A[:, nb:]=jnp.where(r_i==c_i,1.0,0.0)
    sub=lax.broadcasted_iota(jnp.int32,(st,nb),0)
    for s in range(nb//st):
        a=s*st
        TA=A[a:a+st,:nb]; TW=A[a:a+st,nb:]
        B=[jnp.broadcast_to(TA[:,a+c:a+c+1],(st,nb)) for c in range(st)]
        D=jnp.zeros((st,nb),F)
        for c in range(st):
            piv=jnp.broadcast_to(B[c][c:c+1,:],(st,nb))
            D=jnp.where(sub==c,piv,D)
            if c<st-1:
                m=jnp.where(sub>c,B[c]/piv,0.0)
                for e in range(c+1,st):
                    B[e]=B[e]-m*B[e][c:c+1,:]
                TA=TA-m*TA[c:c+1,:]
                TW=TW-m*TW[c:c+1,:]
        q=lax.rsqrt(D)
        VA=TA*q; VW=TW*q
        A[a:a+st,:nb]=VA; A[a:a+st,nb:]=VW
        if s<nb//st-1:
            V=jnp.concatenate([VA,VW],axis=1)
            hi,mid,lo=split3(V)
            hi=hi.astype(F);mid=mid.astype(F);lo=lo.astype(F)
            L=jnp.concatenate([hi,hi,mid,hi,mid,lo],axis=0)[:,:nb].T.astype(BF)
            R=jnp.concatenate([hi,mid,hi,lo,mid,hi],axis=0).astype(BF)
            b=a+st
            A[b:,:]=A[b:,:]-lax.dot_general(L,R,(((1,),(0,)),((),())),preferred_element_type=F)[b:,:]
    return jnp.where(c_i<=r_i,A[:,:nb].T,0.0), jnp.where(c_i<=r_i,A[:,nb:],0.0)


def dot_t(x, y):
    return lax.dot_general(x, y, (((1,), (1,)), ((), ())), precision=lax.Precision.HIGHEST, preferred_element_type=F)


CH = 256
OWN = 1024


def parts_of(width):
    second = 2 * width - 128
    total = (width // 128) * (width // 128 + 1) // 2 * 128
    cuts = [0, 128, width, second, total]
    return [(a, b - a) for a, b in zip(cuts, cuts[1:]) if b > a]


def gram_add(G, T, R, ids):
    reps, width = G.shape[0], R.shape[1]
    M = [jnp.where(ids == b, T, jnp.zeros((), T.dtype)) for b in range(reps)]
    at = 0
    for j in range(width // 256):
        o = 256 * j
        h = width - o
        p = jnp.dot(jnp.concatenate([x[o:, :] for x in M], axis=0), R[:, o : o + 256],
                    preferred_element_type=F)
        for b in range(reps):
            G[b, at : at + h, :] += p[b * h : (b + 1) * h, :128]
            G[b, at + h : at + 2 * h - 128, :] += p[b * h + 128 : (b + 1) * h, 128:]
        at += 2 * h - 128


def exchange_kernel(doms, reps, cap, rows, eblk, lists, hblk, born, own_r, mass, out,
                    S, A, TR, sbuf, rbuf, obuf, hob, G, RB, G2, RB2, OG, bpack, brecv,
                    ssem, rsem, hs, hr, bss, brs, xss, xrs, yss, yrs, oss, ors, lsem):
    p = lax.axis_index("dom")
    q = lax.axis_index("rep")
    me = p * reps + q
    total = doms * reps
    n_rows, width = rows.shape
    nch = sbuf.shape[0]
    PARTS = parts_of(width)
    PIECES = len(PARTS)
    cols = width // 128
    slab = cap * cols
    odd = p % 2
    mate = p + 1 - 2 * odd
    other = p - 1 + 2 * odd
    has_mate = mate < doms
    has_other = (other >= 0) & (other < doms)
    mesh_id = pl.DeviceIdType.MESH

    def halo_copy(ch):
        return pltpu.make_async_remote_copy(
            src_ref=sbuf.at[ch], dst_ref=rbuf.at[ch], send_sem=ssem.at[ch], recv_sem=rsem.at[ch],
            device_id={"dom": mate, "rep": q}, device_id_type=mesh_id)

    def ids_copy():
        return pltpu.make_async_remote_copy(
            src_ref=hblk.at[odd], dst_ref=hob, send_sem=hs, recv_sem=hr,
            device_id={"dom": other, "rep": q}, device_id_type=mesh_id)

    def owner_copy(i):
        at = pl.ds(*PARTS[i])
        return pltpu.make_async_remote_copy(
            src_ref=G2.at[q, at, :], dst_ref=OG.at[at, :], send_sem=oss.at[i], recv_sem=ors.at[i],
            device_id={"dom": other, "rep": q}, device_id_type=mesh_id)

    def stage(Gx, RBx, ss, rs, number, k):
        step, slot = 1, 0
        for _ in range(number):
            slot += reps // (2 * step)
            step *= 2
        bit = (q // step) % 2
        peer = q + step * (1 - 2 * bit)
        low = q % step
        made = []
        for i in range(reps // (2 * step)):
            away = low + (1 - bit) * step + 2 * step * i
            keep = low + bit * step + 2 * step * i
            at = pl.ds(*PARTS[k])
            n = (slot + i) * PIECES + k
            made.append((pltpu.make_async_remote_copy(
                src_ref=Gx.at[away, at, :], dst_ref=RBx.at[slot + i, at, :],
                send_sem=ss.at[n], recv_sem=rs.at[n],
                device_id={"dom": p, "rep": peer}, device_id_type=mesh_id), keep, slot + i))
        return made

    stages = reps.bit_length() - 1
    dsums = (G, RB, xss, xrs)
    osums = (G2, RB2, yss, yrs)

    def stage_start(bufs, number, k):
        for cp, _, _ in stage(*bufs, number, k):
            cp.start()

    def stage_finish(bufs, number, k):
        Gx, RBx = bufs[0], bufs[1]
        at = pl.ds(*PARTS[k])
        for cp, keep, slot in stage(*bufs, number, k):
            cp.wait_recv()
            Gx[keep, at, :] += RBx[slot, at, :]

    def stage_through(bufs):
        for number in range(stages - 1):
            for k in range(PIECES):
                stage_finish(bufs, number, k)
                stage_start(bufs, number + 1, k)

    barrier = pltpu.get_barrier_semaphore()

    def greet(k, _):
        to = (me + k) % total
        pl.semaphore_signal(barrier, inc=1, device_id={"dom": to // reps, "rep": to % reps}, device_id_type=mesh_id)
        return 0

    lax.fori_loop(1, total, greet, 0)

    for c in range(n_rows // CH):
        TR[:, c * CH : (c + 1) * CH] = rows[c * CH : (c + 1) * CH, :].T
    G2[...] = jnp.zeros_like(G2)

    def picked(half, ch):
        l = lists[:, pl.ds(pl.multiple_of((half * nch + ch) * CH, CH), CH)]
        i = lax.broadcasted_iota(jnp.int32, (n_rows, CH), 0)
        PT = jnp.where(i == l, 1.0, 0.0).astype(BF)
        return jnp.dot(TR[...], PT, preferred_element_type=F).astype(BF)

    def add_blocks(Gx, T, R, ids):
        gram_add(Gx, T, R, ids)

    @pl.when(has_mate)
    def _():
        sbuf[0] = picked(1 - odd, 0)

    pl.semaphore_wait(barrier, total - 1)

    @pl.when(has_other)
    def _():
        ids_copy().start()

    @pl.when(has_mate)
    def _():
        halo_copy(0).start()

    AHEAD = min(2, nch)

    @pl.when(has_mate)
    def _():
        for ch in range(1, AHEAD):
            sbuf[ch] = picked(1 - odd, ch)
            halo_copy(ch).start()

    @pl.when(has_other)
    def _():
        ids_copy().wait_recv()

    def gather_step(ch, _):
        @pl.when(has_other)
        def _():
            obuf[...] = picked(odd, ch)
            T = obuf[...]
            add_blocks(G2, T, T.T, hob[:, pl.ds(pl.multiple_of(ch * CH, CH), CH)])

        @pl.when(has_mate & (ch < nch - AHEAD))
        def _():
            sbuf[ch + AHEAD] = picked(1 - odd, ch + AHEAD)
            halo_copy(ch + AHEAD).start()
        return 0

    lax.fori_loop(0, nch, gather_step, 0)

    @pl.when(has_other)
    def _():
        for k in range(PIECES):
            stage_start(osums, 0, k)

    n_born = born.shape[0]
    ii = lax.broadcasted_iota(jnp.int32, (n_born, n_born), 0)
    jj = lax.broadcasted_iota(jnp.int32, (n_born, n_born), 1)
    own = jnp.broadcast_to(own_r[...].astype(F), (n_born, n_born))
    same = (own.T == own) & (ii < jj)
    rank = jnp.sum(jnp.where(same, 1.0, 0.0), axis=0, keepdims=True).astype(jnp.int32)
    base = own_r[...] * slab + rank * cols
    m = lax.broadcasted_iota(jnp.int32, (total * slab, n_born), 0)
    acc = jnp.zeros((total * slab, 128), F)
    for c in range(cols):
        oh = jnp.where(m == base + c, 1.0, 0.0).astype(BF)
        acc += jnp.dot(oh, born[:, c * 128 : (c + 1) * 128], preferred_element_type=F)
    bpack[...] = acc.astype(BF)

    def born_copy(to, frm):
        return pltpu.make_async_remote_copy(
            src_ref=bpack.at[pl.ds(pl.multiple_of(to * slab, slab), slab), :],
            dst_ref=brecv.at[pl.ds(pl.multiple_of(frm * slab, slab), slab), :],
            send_sem=bss.at[to], recv_sem=brs.at[frm],
            device_id={"dom": to // reps, "rep": to % reps}, device_id_type=mesh_id)

    def born_send(k, _):
        to = (me + k) % total
        born_copy(to, me).start()
        return 0

    lax.fori_loop(1, total, born_send, 0)
    mine = pl.ds(pl.multiple_of(me * slab, slab), slab)
    local = pltpu.make_async_copy(bpack.at[mine, :], brecv.at[mine, :], lsem)
    local.start()

    @pl.when(has_other)
    def _():
        stage_through(osums)

    G[...] = jnp.zeros_like(G)

    def own_step(c, _):
        at = pl.ds(pl.multiple_of(c * OWN, OWN), OWN)
        add_blocks(G, TR[:, at], rows[at, :], eblk[:, at])
        return 0

    lax.fori_loop(0, n_rows // OWN, own_step, 0)

    def halo_step(ch, _):
        @pl.when(has_mate)
        def _():
            halo_copy(ch).wait_recv()
            T = rbuf[ch]
            add_blocks(G, T, T.T, hblk[1 - odd, :, pl.ds(pl.multiple_of(ch * CH, CH), CH)])
        return 0

    lax.fori_loop(0, nch, halo_step, 0)

    for k in range(PIECES):
        stage_start(dsums, 0, k)
    stage_through(dsums)

    @pl.when(has_other)
    def _():
        for k in range(PIECES):
            stage_finish(osums, stages - 1, k)
            owner_copy(k).start()

    def born_wait(k, _):
        frm = (me + k) % total
        born_copy(frm, frm).wait_recv()
        return 0

    lax.fori_loop(1, total, born_wait, 0)
    local.wait()
    n = total * cap
    mm = lax.broadcasted_iota(jnp.int32, (n, total * slab), 0)
    kk = lax.broadcasted_iota(jnp.int32, (n, total * slab), 1)
    Bv = brecv[...]
    V = jnp.concatenate(
        [jnp.dot(jnp.where(kk == mm * cols + c, 1.0, 0.0).astype(BF), Bv, preferred_element_type=F)
         for c in range(cols)], axis=1)
    VT = V.T.astype(BF)
    V = V.astype(BF)
    r_i = lax.broadcasted_iota(jnp.int32, (128, 128), 0)
    c_i = lax.broadcasted_iota(jnp.int32, (128, 128), 1)
    scale = 1.0 / width
    for j in range(cols):
        o = 128 * j
        S[o:, o : o + 128] = scale * jnp.dot(VT[o:, :], V[:, o : o + 128], preferred_element_type=F)
        S[o : o + 128, o : o + 128] += jnp.where(r_i == c_i, mass[:, o : o + 128], 0.0)

    def take(k):
        first, count = PARTS[k]
        spans, at = [], 0
        for j in range(cols):
            lo, hi = max(first, at), min(first + count, at + width - 128 * j)
            if lo < hi:
                spans.append((lo, hi - lo, 128 * j + lo - at, 128 * j))
            at += width - 128 * j

        def add(plus):
            for lo, n, r, c in spans:
                S[r : r + n, c : c + 128] += scale * plus(pl.ds(lo, n))

        @pl.when(has_other)
        def _():
            owner_copy(k).wait_recv()
            add(lambda at: OG[at, :])

        for cp, _, slot in stage(*dsums, stages - 1, k):
            cp.wait_recv()
            add(lambda at: G[q, at, :] + RB[slot, at, :])

    edges, at = [], 0
    for j in range(cols):
        edges.append((at, at + 128, at + width - 128 * j))
        at += width - 128 * j
    taken = 0

    def take_to(row):
        nonlocal taken
        while taken < PIECES and PARTS[taken][0] < row:
            take(taken)
            taken += 1

    for j in range(cols):
        o = 128 * j
        take_to(edges[j][1])
        Ld, W = chol_diag(S[o : o + 128, o : o + 128], A)
        out[o : o + 128, o : o + 128] = Ld
        if j < cols - 1:
            out[o : o + 128, o + 128 :] = jnp.zeros((128, width - o - 128), F)
            take_to(edges[j][2])
            L21 = dot_t(S[o + 128 :, o : o + 128], W)
            out[o + 128 :, o : o + 128] = L21
            S[o + 128 :, o + 128 :] = S[o + 128 :, o + 128 :] - dot_t(L21, L21)

    def stages_done(bufs):
        for number in range(stages):
            for k in range(PIECES):
                for cp, _, _ in stage(*bufs, number, k):
                    cp.wait_send()

    stages_done(dsums)

    @pl.when(has_other)
    def _():
        ids_copy().wait_send()
        stages_done(osums)
        for k in range(PIECES):
            owner_copy(k).wait_send()

    def born_done(k, _):
        to = (me + k) % total
        born_copy(to, me).wait_send()
        return 0

    lax.fori_loop(1, total, born_done, 0)

    def halo_done(ch, _):
        @pl.when(has_mate)
        def _():
            halo_copy(ch).wait_send()
        return 0

    lax.fori_loop(0, nch, halo_done, 0)


def solution(mesh):
    doms, reps = mesh.shape["dom"], mesh.shape["rep"]
    total = doms * reps

    def local(elem_rows, elem_block, send_lists, halo_block, born_rows, born_owner, mass):
        n_rows, width = elem_rows.shape
        half = send_lists.shape[0] // 2
        nch = half // CH
        tri = (width // 128) * (width // 128 + 1) // 2 * 128
        slab = CAP * (width // 128)
        PIECES = len(parts_of(width))
        vm = pl.BlockSpec(memory_space=pltpu.VMEM)
        return pl.pallas_call(
            functools.partial(exchange_kernel, doms, reps, CAP),
            out_shape=jax.ShapeDtypeStruct((width, width), F),
            in_specs=[vm] * 7,
            out_specs=vm,
            scratch_shapes=[
                pltpu.VMEM((width, width), F),
                pltpu.VMEM((128, 256), F),
                pltpu.VMEM((width, n_rows), BF),
                pltpu.VMEM((nch, width, CH), BF),
                pltpu.VMEM((nch, width, CH), BF),
                pltpu.VMEM((width, CH), BF),
                pltpu.VMEM((1, half), jnp.int32),
                pltpu.VMEM((reps, tri, 128), F),
                pltpu.VMEM((reps - 1, tri, 128), F),
                pltpu.VMEM((reps, tri, 128), F),
                pltpu.VMEM((reps - 1, tri, 128), F),
                pltpu.VMEM((tri, 128), F),
                pltpu.VMEM((total * slab, 128), BF),
                pltpu.VMEM((total * slab, 128), BF),
                pltpu.SemaphoreType.DMA((nch,)),
                pltpu.SemaphoreType.DMA((nch,)),
                pltpu.SemaphoreType.DMA,
                pltpu.SemaphoreType.DMA,
                pltpu.SemaphoreType.DMA((total,)),
                pltpu.SemaphoreType.DMA((total,)),
                pltpu.SemaphoreType.DMA(((reps - 1) * PIECES,)),
                pltpu.SemaphoreType.DMA(((reps - 1) * PIECES,)),
                pltpu.SemaphoreType.DMA(((reps - 1) * PIECES,)),
                pltpu.SemaphoreType.DMA(((reps - 1) * PIECES,)),
                pltpu.SemaphoreType.DMA((PIECES,)),
                pltpu.SemaphoreType.DMA((PIECES,)),
                pltpu.SemaphoreType.DMA,
            ],
            compiler_params=pltpu.CompilerParams(collective_id=0, has_side_effects=True, vmem_limit_bytes=48 * 1024 * 1024),
        )(elem_rows, elem_block[None, :], send_lists[None, :], halo_block.reshape(2, 1, half),
          born_rows, born_owner.reshape(1, -1), mass[None, :])

    both = P(("dom", "rep"))
    rows2 = P(("dom", "rep"), None)
    return jax.shard_map(local, mesh=mesh, in_specs=(rows2, both, both, both, rows2, rows2, both),
                         out_specs=rows2, check_vma=False)
```

```python
import functools

import jax
import jax.numpy as jnp
from jax import lax
from jax.experimental import pallas as pl
from jax.experimental.pallas import tpu as pltpu
from jax.sharding import PartitionSpec as P

CAP = 4
F=jnp.float32; BF=jnp.bfloat16

def split3(v):
    hi=v.astype(BF); r=v-hi.astype(F); mid=r.astype(BF); lo=(r-mid.astype(F)).astype(BF)
    return hi,mid,lo

def chol_diag(D, A):
    nb=D.shape[0]; st=16
    r_i=lax.broadcasted_iota(jnp.int32,(nb,nb),0); c_i=lax.broadcasted_iota(jnp.int32,(nb,nb),1)
    A[:, :nb]=D
    A[:, nb:]=jnp.where(r_i==c_i,1.0,0.0)
    sub=lax.broadcasted_iota(jnp.int32,(st,nb),0)
    for s in range(nb//st):
        a=s*st
        TA=A[a:a+st,:nb]; TW=A[a:a+st,nb:]
        B=[jnp.broadcast_to(TA[:,a+c:a+c+1],(st,nb)) for c in range(st)]
        D=jnp.zeros((st,nb),F)
        for c in range(st):
            piv=jnp.broadcast_to(B[c][c:c+1,:],(st,nb))
            D=jnp.where(sub==c,piv,D)
            if c<st-1:
                m=jnp.where(sub>c,B[c]/piv,0.0)
                for e in range(c+1,st):
                    B[e]=B[e]-m*B[e][c:c+1,:]
                TA=TA-m*TA[c:c+1,:]
                TW=TW-m*TW[c:c+1,:]
        q=lax.rsqrt(D)
        VA=TA*q; VW=TW*q
        A[a:a+st,:nb]=VA; A[a:a+st,nb:]=VW
        if s<nb//st-1:
            V=jnp.concatenate([VA,VW],axis=1)
            hi,mid,lo=split3(V)
            hi=hi.astype(F);mid=mid.astype(F);lo=lo.astype(F)
            L=jnp.concatenate([hi,hi,mid,hi,mid,lo],axis=0)[:,:nb].T.astype(BF)
            R=jnp.concatenate([hi,mid,hi,lo,mid,hi],axis=0).astype(BF)
            b=a+st
            A[b:,:]=A[b:,:]-lax.dot_general(L,R,(((1,),(0,)),((),())),preferred_element_type=F)[b:,:]
    return jnp.where(c_i<=r_i,A[:,:nb].T,0.0), jnp.where(c_i<=r_i,A[:,nb:],0.0)


def dot_t(x, y):
    return lax.dot_general(x, y, (((1,), (1,)), ((), ())), precision=lax.Precision.HIGHEST, preferred_element_type=F)


CH = 256
OWN = 1024


def layout(width):
    cols = width // 128
    diag, rest, parts, at = {1: 0, 0: 128}, {0: 256}, [(120, 136), (256, width - 128)], 128 + width
    for j in range(2, cols, 2):
        rest[j - 1], diag[j] = at, at + width - 128 * j
        parts.append((at, width - 128 * (j - 1)))
        at += width - 128 * (j - 1)
        rest[j] = at
        parts.append((at, width - 128 * (j + 1)))
        at += width - 128 * (j + 1)
    rest[cols - 1] = at
    for j in range(3, cols, 2):
        diag[j] = at
        at += 128
    return diag, rest, parts, at


def gram_add(G, T, R, ids):
    reps, width = G.shape[0], R.shape[1]
    diag, rest, _, _ = layout(width)
    M = [jnp.where(ids == b, T, jnp.zeros((), T.dtype)) for b in range(reps)]
    for j in range(0, width // 128, 2):
        o = 128 * j
        h = width - o
        p = jnp.dot(jnp.concatenate([x[o:, :] for x in M], axis=0), R[:, o : o + 256],
                    preferred_element_type=F)
        for b in range(reps):
            y = p[b * h : (b + 1) * h, :]
            G[b, diag[j] : diag[j] + 128, :] += y[:128, :128]
            G[b, rest[j] : rest[j] + h - 128, :] += y[128:, :128]
            G[b, diag[j + 1] : diag[j + 1] + 128, :] += y[128:256, 128:]
            if h > 256:
                G[b, rest[j + 1] : rest[j + 1] + h - 256, :] += y[256:, 128:]


def pack_diagonals(G, r_i, c_i):
    width = 128
    cols = 1
    while layout_rows(cols) < G.shape[1]:
        cols += 1
    diag, _, _, _ = layout(width * cols)
    for b in range(G.shape[0]):
        ends = []
        for j in range(0, cols, 2):
            low, up = slice(diag[j], diag[j] + 128), slice(diag[j + 1], diag[j + 1] + 128)
            Y = G[b, up, :]
            ends.append(jnp.sum(jnp.where(r_i == c_i, Y, 0.0), axis=0, keepdims=True))
            G[b, low, :] = jnp.where(c_i <= r_i, G[b, low, :], Y)
        pad = jnp.zeros((8 - len(ends), 128), F)
        G[b, 120:128, :] = jnp.concatenate(ends + [pad], axis=0)


def layout_rows(cols):
    return cols * (cols + 1) // 2 * 128


def exchange_kernel(doms, reps, cap, rows, eblk, lists, hblk, born, own_r, mass, out,
                    S, A, DG, TR, sbuf, rbuf, obuf, hob, G, RB, G2, RB2, OG, bpack, brecv,
                    ssem, rsem, hs, hr, bss, brs, xss, xrs, yss, yrs, oss, ors, lsem, near, met):
    p = lax.axis_index("dom")
    q = lax.axis_index("rep")
    me = p * reps + q
    total = doms * reps
    n_rows, width = rows.shape
    nch = sbuf.shape[0]
    diag, rest, parts, _ = layout(width)
    pieces = len(parts)
    cols = width // 128
    slab = cap * cols
    odd = p % 2
    mate = p + 1 - 2 * odd
    other = p - 1 + 2 * odd
    has_mate = mate < doms
    has_other = (other >= 0) & (other < doms)
    mesh_id = pl.DeviceIdType.MESH
    r_i = lax.broadcasted_iota(jnp.int32, (128, 128), 0)
    c_i = lax.broadcasted_iota(jnp.int32, (128, 128), 1)
    steps = [1 << i for i in range(reps.bit_length() - 1)]
    stages = len(steps)

    def flip(step):
        return q + step * (1 - 2 * ((q // step) % 2))

    def signal(sem, dom, rep):
        pl.semaphore_signal(sem, inc=1, device_id={"dom": dom, "rep": rep}, device_id_type=mesh_id)

    def halo_copy(ch):
        return pltpu.make_async_remote_copy(
            src_ref=sbuf.at[ch], dst_ref=rbuf.at[ch], send_sem=ssem.at[ch], recv_sem=rsem.at[ch],
            device_id={"dom": mate, "rep": q}, device_id_type=mesh_id)

    def ids_copy():
        return pltpu.make_async_remote_copy(
            src_ref=hblk.at[odd], dst_ref=hob, send_sem=hs, recv_sem=hr,
            device_id={"dom": other, "rep": q}, device_id_type=mesh_id)

    def owner_copy(i):
        at = pl.ds(*parts[i])
        return pltpu.make_async_remote_copy(
            src_ref=G2.at[q, at, :], dst_ref=OG.at[at, :], send_sem=oss.at[i], recv_sem=ors.at[i],
            device_id={"dom": other, "rep": q}, device_id_type=mesh_id)

    def stage(Gx, RBx, ss, rs, number, k):
        slot = 0
        for step in steps[:number]:
            slot += reps // (2 * step)
        step = steps[number]
        bit = (q // step) % 2
        low = q % step
        made = []
        for i in range(reps // (2 * step)):
            away = low + (1 - bit) * step + 2 * step * i
            keep = low + bit * step + 2 * step * i
            at = pl.ds(*parts[k])
            n = (slot + i) * pieces + k
            made.append((pltpu.make_async_remote_copy(
                src_ref=Gx.at[away, at, :], dst_ref=RBx.at[slot + i, at, :],
                send_sem=ss.at[n], recv_sem=rs.at[n],
                device_id={"dom": p, "rep": flip(step)}, device_id_type=mesh_id), keep, slot + i))
        return made

    dsums = (G, RB, xss, xrs)
    osums = (G2, RB2, yss, yrs)

    def stage_start(bufs, number, k):
        for cp, _, _ in stage(*bufs, number, k):
            cp.start()

    def stage_finish(bufs, number, k):
        Gx, RBx = bufs[0], bufs[1]
        at = pl.ds(*parts[k])
        for cp, keep, slot in stage(*bufs, number, k):
            cp.wait_recv()
            Gx[keep, at, :] += RBx[slot, at, :]

    def stage_through(bufs):
        for number in range(stages - 1):
            for k in range(pieces):
                stage_finish(bufs, number, k)
                stage_start(bufs, number + 1, k)

    def stages_done(bufs):
        for number in range(stages):
            for k in range(pieces):
                for cp, _, _ in stage(*bufs, number, k):
                    cp.wait_send()

    barrier = pltpu.get_barrier_semaphore()
    for step in steps:
        signal(barrier, p, flip(step))

    @pl.when(has_mate)
    def _():
        signal(barrier, mate, q)

    @pl.when(has_other)
    def _():
        signal(barrier, other, q)

    for c in range(n_rows // CH):
        TR[:, c * CH : (c + 1) * CH] = rows[c * CH : (c + 1) * CH, :].T

    def picked(half, ch):
        l = lists[:, pl.ds(pl.multiple_of((half * nch + ch) * CH, CH), CH)]
        i = lax.broadcasted_iota(jnp.int32, (n_rows, CH), 0)
        PT = jnp.where(i == l, 1.0, 0.0).astype(BF)
        return jnp.dot(TR[...], PT, preferred_element_type=F).astype(BF)

    @pl.when(has_mate)
    def _():
        sbuf[0] = picked(1 - odd, 0)

    pl.semaphore_wait(barrier, stages + jnp.where(has_mate, 1, 0) + jnp.where(has_other, 1, 0))

    @pl.when(has_mate)
    def _():
        halo_copy(0).start()

    @pl.when(has_other)
    def _():
        ids_copy().start()

    def meet(i, d, then_wait):
        up, down = p + d < doms, p - d >= 0
        if then_wait:
            pl.semaphore_wait(near.at[i], jnp.where(up, 1, 0) + jnp.where(down, 1, 0))
            return

        @pl.when(up)
        def _():
            signal(near.at[i], p + d, q)

        @pl.when(down)
        def _():
            signal(near.at[i], p - d, q)

    rounds = (doms - 1).bit_length()
    ahead = min(2, nch)
    early = min(rounds, nch)

    @pl.when(has_mate)
    def _():
        for ch in range(1, ahead):
            sbuf[ch] = picked(1 - odd, ch)
            halo_copy(ch).start()

    G2[...] = jnp.zeros_like(G2)
    G[...] = jnp.zeros_like(G)

    @pl.when(has_other)
    def _():
        ids_copy().wait_recv()

    @pl.when(jnp.logical_not(has_other))
    def _():
        OG[...] = jnp.zeros_like(OG)

    def gather_step(ch, d):
        @pl.when(ch < early)
        def _():
            meet(ch, d, False)

        @pl.when(has_other)
        def _():
            obuf[...] = picked(odd, ch)
            T = obuf[...]
            gram_add(G2, T, T.T, hob[:, pl.ds(pl.multiple_of(ch * CH, CH), CH)])

        @pl.when(has_mate & (ch < nch - ahead))
        def _():
            sbuf[ch + ahead] = picked(1 - odd, ch + ahead)
            halo_copy(ch + ahead).start()

        @pl.when(ch < early)
        def _():
            meet(ch, d, True)
        return 2 * d

    lax.fori_loop(0, nch, gather_step, 1)

    @pl.when(has_other)
    def _():
        pack_diagonals(G2, r_i, c_i)
        for k in range(pieces):
            stage_start(osums, 0, k)

    for i in range(early, rounds):
        meet(i, 1 << i, False)
        meet(i, 1 << i, True)
    for i, step in enumerate(steps):
        signal(met.at[i], p, flip(step))
        if i == 0:
            n_born = born.shape[0]
            ii = lax.broadcasted_iota(jnp.int32, (n_born, n_born), 0)
            jj = lax.broadcasted_iota(jnp.int32, (n_born, n_born), 1)
            own = jnp.broadcast_to(own_r[...].astype(F), (n_born, n_born))
            same = (own.T == own) & (ii < jj)
            rank = jnp.sum(jnp.where(same, 1.0, 0.0), axis=0, keepdims=True).astype(jnp.int32)
            base = own_r[...] * slab + rank * cols
            m = lax.broadcasted_iota(jnp.int32, (total * slab, n_born), 0)
            acc = jnp.zeros((total * slab, 128), F)
            for c in range(cols):
                oh = jnp.where(m == base + c, 1.0, 0.0).astype(BF)
                acc += jnp.dot(oh, born[:, c * 128 : (c + 1) * 128], preferred_element_type=F)
            bpack[...] = acc.astype(BF)
        pl.semaphore_wait(met.at[i], 1)

        if i == 0:
            @pl.when(has_other)
            def _():
                stage_through(osums)

    def born_copy(to, frm):
        return pltpu.make_async_remote_copy(
            src_ref=bpack.at[pl.ds(pl.multiple_of(to * slab, slab), slab), :],
            dst_ref=brecv.at[pl.ds(pl.multiple_of(frm * slab, slab), slab), :],
            send_sem=bss.at[to], recv_sem=brs.at[frm],
            device_id={"dom": to // reps, "rep": to % reps}, device_id_type=mesh_id)

    def born_send(k, _):
        to = (me + k) % total
        born_copy(to, me).start()
        return 0

    lax.fori_loop(1, total, born_send, 0)
    mine = pl.ds(pl.multiple_of(me * slab, slab), slab)
    local = pltpu.make_async_copy(bpack.at[mine, :], brecv.at[mine, :], lsem)
    local.start()

    def own_step(c, _):
        at = pl.ds(pl.multiple_of(c * OWN, OWN), OWN)
        gram_add(G, TR[:, at], rows[at, :], eblk[:, at])
        return 0

    lax.fori_loop(0, n_rows // OWN, own_step, 0)

    def born_wait(k, _):
        frm = (me + k) % total
        born_copy(frm, frm).wait_recv()
        return 0

    def add_born():
        lax.fori_loop(1, total, born_wait, 0)
        local.wait()
        n = total * cap
        mm = lax.broadcasted_iota(jnp.int32, (n, total * slab), 0)
        kk = lax.broadcasted_iota(jnp.int32, (n, total * slab), 1)
        Bv = brecv[...]
        V = jnp.concatenate(
            [jnp.dot(jnp.where(kk == mm * cols + c, 1.0, 0.0).astype(BF), Bv, preferred_element_type=F)
             for c in range(cols)], axis=1)
        VT = V.T.astype(BF)
        V = V.astype(BF)
        for j in range(cols):
            o = 128 * j
            S[o:, o : o + 128] = scale * jnp.dot(VT[o:, :], V[:, o : o + 128], preferred_element_type=F)
            S[o : o + 128, o : o + 128] += jnp.where(r_i == c_i, mass[:, o : o + 128], 0.0)

    scale = 1.0 / width

    def halo_step(ch, _):
        @pl.when(has_mate)
        def _():
            halo_copy(ch).wait_recv()

        @pl.when(has_other & (ch == nch - 1))
        def _():
            for k in range(pieces):
                owner_copy(k).start()

        @pl.when(has_mate)
        def _():
            T = rbuf[ch]
            gram_add(G, T, T.T, hblk[1 - odd, :, pl.ds(pl.multiple_of(ch * CH, CH), CH)])

        @pl.when(ch == LATE)
        def _():
            add_born()

            @pl.when(has_other)
            def _():
                for k in range(pieces):
                    stage_finish(osums, stages - 1, k)
        return 0

    LATE = max(nch - 2, 0)
    lax.fori_loop(0, nch, halo_step, 0)

    pack_diagonals(G, r_i, c_i)
    for k in range(pieces):
        stage_start(dsums, 0, k)
    stage_through(dsums)

    def take(k):
        at = pl.ds(*parts[k])
        (cp, _, slot), = stage(*dsums, stages - 1, k)
        cp.wait_recv()

        @pl.when(has_other)
        def _():
            owner_copy(k).wait_recv()

        def value(first, count):
            at = pl.ds(first, count)
            return scale * (G[q, at, :] + RB[slot, at, :] + OG[at, :])

        def pair(j):
            X = value(diag[j], 128)
            XT = X.T
            ends = DG[j // 2 : j // 2 + 1, :]
            S[128 * j : 128 * j + 128, 128 * j : 128 * j + 128] += jnp.where(c_i <= r_i, X, XT)
            o = 128 * j + 128
            S[o : o + 128, o : o + 128] += jnp.where(c_i > r_i, X, jnp.where(c_i < r_i, XT, ends))

        def column(j):
            o = 128 * j
            S[o + 128 :, o : o + 128] += value(rest[j], width - o - 128)

        if k == 0:
            DG[...] = value(120, 8)
            pair(0)
        elif k % 2 == 0:
            column(k - 1)
            pair(k)
        else:
            column(k - 1)

    def take_to(last):
        nonlocal taken
        while taken <= last:
            take(taken)
            taken += 1

    taken = 0
    for j in range(cols):
        o = 128 * j
        take_to(j - j % 2)
        Ld, W = chol_diag(S[o : o + 128, o : o + 128], A)
        out[o : o + 128, o : o + 128] = Ld
        if j < cols - 1:
            out[o : o + 128, o + 128 :] = jnp.zeros((128, width - o - 128), F)
            take_to(j + 1)
            L21 = dot_t(S[o + 128 :, o : o + 128], W)
            out[o + 128 :, o : o + 128] = L21
            S[o + 128 :, o + 128 :] = S[o + 128 :, o + 128 :] - dot_t(L21, L21)

    stages_done(dsums)

    @pl.when(has_other)
    def _():
        ids_copy().wait_send()
        stages_done(osums)
        for k in range(pieces):
            owner_copy(k).wait_send()

    def born_done(k, _):
        to = (me + k) % total
        born_copy(to, me).wait_send()
        return 0

    lax.fori_loop(1, total, born_done, 0)

    def halo_done(ch, _):
        @pl.when(has_mate)
        def _():
            halo_copy(ch).wait_send()
        return 0

    lax.fori_loop(0, nch, halo_done, 0)


def solution(mesh):
    doms, reps = mesh.shape["dom"], mesh.shape["rep"]
    total = doms * reps

    def local(elem_rows, elem_block, send_lists, halo_block, born_rows, born_owner, mass):
        n_rows, width = elem_rows.shape
        half = send_lists.shape[0] // 2
        nch = half // CH
        _, _, parts, tri = layout(width)
        pieces = len(parts)
        slab = CAP * (width // 128)
        rounds = max(1, (doms - 1).bit_length())
        stages = max(1, reps.bit_length() - 1)
        dma = pltpu.SemaphoreType.DMA
        vm = pl.BlockSpec(memory_space=pltpu.VMEM)
        return pl.pallas_call(
            functools.partial(exchange_kernel, doms, reps, CAP),
            out_shape=jax.ShapeDtypeStruct((width, width), F),
            in_specs=[vm] * 7,
            out_specs=vm,
            scratch_shapes=[
                pltpu.VMEM((width, width), F),
                pltpu.VMEM((128, 256), F),
                pltpu.VMEM((8, 128), F),
                pltpu.VMEM((width, n_rows), BF),
                pltpu.VMEM((nch, width, CH), BF),
                pltpu.VMEM((nch, width, CH), BF),
                pltpu.VMEM((width, CH), BF),
                pltpu.VMEM((1, half), jnp.int32),
                pltpu.VMEM((reps, tri, 128), F),
                pltpu.VMEM((reps - 1, tri, 128), F),
                pltpu.VMEM((reps, tri, 128), F),
                pltpu.VMEM((reps - 1, tri, 128), F),
                pltpu.VMEM((tri, 128), F),
                pltpu.VMEM((total * slab, 128), BF),
                pltpu.VMEM((total * slab, 128), BF),
                dma((nch,)),
                dma((nch,)),
                dma,
                dma,
                dma((total,)),
                dma((total,)),
                dma(((reps - 1) * pieces,)),
                dma(((reps - 1) * pieces,)),
                dma(((reps - 1) * pieces,)),
                dma(((reps - 1) * pieces,)),
                dma((pieces,)),
                dma((pieces,)),
                dma,
                pltpu.SemaphoreType.REGULAR((rounds,)),
                pltpu.SemaphoreType.REGULAR((stages,)),
            ],
            compiler_params=pltpu.CompilerParams(
                collective_id=0, has_side_effects=True, vmem_limit_bytes=63 * 1024 * 1024),
        )(elem_rows, elem_block[None, :], send_lists[None, :], halo_block.reshape(2, 1, half),
          born_rows, born_owner.reshape(1, -1), mass[None, :])

    both = P(("dom", "rep"))
    rows2 = P(("dom", "rep"), None)
    return jax.shard_map(local, mesh=mesh, in_specs=(rows2, both, both, both, rows2, rows2, both),
                         out_specs=rows2, check_vma=False)
```

```python
import functools

import jax
import jax.numpy as jnp
from jax import lax
from jax.experimental import pallas as pl
from jax.experimental.pallas import tpu as pltpu
from jax.sharding import PartitionSpec as P

CAP = 4
F=jnp.float32; BF=jnp.bfloat16

def split3(v):
    hi=v.astype(BF); r=v-hi.astype(F); mid=r.astype(BF); lo=(r-mid.astype(F)).astype(BF)
    return hi,mid,lo

def chol_diag(D, A):
    nb=D.shape[0]; st=16
    r_i=lax.broadcasted_iota(jnp.int32,(nb,nb),0); c_i=lax.broadcasted_iota(jnp.int32,(nb,nb),1)
    A[:, :nb]=D
    A[:, nb:]=jnp.where(r_i==c_i,1.0,0.0)
    sub=lax.broadcasted_iota(jnp.int32,(st,nb),0)
    TA=A[0:st,:nb]; TW=A[0:st,nb:]
    for s in range(nb//st):
        a=s*st
        B=[jnp.broadcast_to(TA[:,a+c:a+c+1],(st,nb)) for c in range(st)]
        D=jnp.zeros((st,nb),F)
        for c in range(st):
            piv=jnp.broadcast_to(B[c][c:c+1,:],(st,nb))
            D=jnp.where(sub==c,piv,D)
            if c<st-1:
                m=jnp.where(sub>c,B[c]/piv,0.0)
                for e in range(c+1,st):
                    B[e]=B[e]-m*B[e][c:c+1,:]
                TA=TA-m*TA[c:c+1,:]
                TW=TW-m*TW[c:c+1,:]
        q=lax.rsqrt(D)
        VA=TA*q; VW=TW*q
        A[a:a+st,:nb]=VA; A[a:a+st,nb:]=VW
        if s<nb//st-1:
            hi,mid,lo=split3(jnp.concatenate([VA,VW],axis=1))
            L=jnp.concatenate([hi,hi,mid,hi,mid,lo],axis=0)[:,:nb].T
            R=jnp.concatenate([hi,mid,hi,lo,mid,hi],axis=0)
            b=a+st; e=b+st
            N=A[b:e,:]-jnp.dot(L[b:e],R,preferred_element_type=F)
            TA=N[:,:nb]; TW=N[:,nb:]
            if e<nb:
                A[e:,:]=A[e:,:]-jnp.dot(L[e:],R,preferred_element_type=F)
    return jnp.where(c_i<=r_i,A[:,:nb].T,0.0), jnp.where(c_i<=r_i,A[:,nb:],0.0)


def dot_t(x, y):
    xh, xm, xl = split3(x)
    yh, ym, yl = split3(y)
    return lax.dot_general(jnp.concatenate([xh, xh, xm, xh, xm, xl], axis=1),
                           jnp.concatenate([yh, ym, yh, yl, ym, yh], axis=1),
                           (((1,), (1,)), ((), ())), preferred_element_type=F)


CH = 256


def layout(width):
    cols = width // 128
    diag, rest, parts, at = {1: 0, 0: 128}, {0: 256}, [(120, 136), (256, width - 128)], 128 + width
    for j in range(2, cols, 2):
        rest[j - 1], diag[j] = at, at + width - 128 * j
        parts.append((at, width - 128 * (j - 1)))
        at += width - 128 * (j - 1)
        rest[j] = at
        parts.append((at, width - 128 * (j + 1)))
        at += width - 128 * (j + 1)
    rest[cols - 1] = at
    for j in range(3, cols, 2):
        diag[j] = at
        at += 128
    return diag, rest, parts, at


def gram(G, T, R, ids, add):
    reps, width = G.shape[0], R.shape[1]
    diag, rest, _, _ = layout(width)
    M = [jnp.where(ids == b, T, jnp.zeros((), T.dtype)) for b in range(reps)]

    def put(b, first, y):
        at = pl.ds(first, y.shape[0])
        if add:
            G[b, at, :] += y
        else:
            G[b, at, :] = y

    for j in range(0, width // 128, 2):
        o = 128 * j
        h = width - o
        p = jnp.dot(jnp.concatenate([x[o:, :] for x in M], axis=0), R[:, o : o + 256],
                    preferred_element_type=F)
        for b in range(reps):
            y = p[b * h : (b + 1) * h, :]
            put(b, diag[j], y[:128, :128])
            put(b, rest[j], y[128:, :128])
            put(b, diag[j + 1], y[128:256, 128:])
            if h > 256:
                put(b, rest[j + 1], y[256:, 128:])


def pack_diagonals(G, r_i, c_i):
    width = 128
    cols = 1
    while layout_rows(cols) < G.shape[1]:
        cols += 1
    diag, _, _, _ = layout(width * cols)
    for b in range(G.shape[0]):
        ends = []
        for j in range(0, cols, 2):
            low, up = slice(diag[j], diag[j] + 128), slice(diag[j + 1], diag[j + 1] + 128)
            Y = G[b, up, :]
            ends.append(jnp.sum(jnp.where(r_i == c_i, Y, 0.0), axis=0, keepdims=True))
            G[b, low, :] = jnp.where(c_i <= r_i, G[b, low, :], Y)
        pad = jnp.zeros((8 - len(ends), 128), F)
        G[b, 120:128, :] = jnp.concatenate(ends + [pad], axis=0)


def layout_rows(cols):
    return cols * (cols + 1) // 2 * 128


def exchange_kernel(doms, reps, cap, rows, eblk, lists, hblk, born, own_r, mass, out,
                    S, A, DG, TR, sbuf, rbuf, lids, hob, G, RB, G2, RB2, OG, bpack, brecv,
                    ssem, rsem, hs, hr, bss, brs, xss, xrs, yss, yrs, oss, ors, lsem, near, met):
    p = lax.axis_index("dom")
    q = lax.axis_index("rep")
    me = p * reps + q
    total = doms * reps
    n_rows, width = rows.shape
    nch = ssem.shape[0]
    diag, rest, parts, _ = layout(width)
    pieces = len(parts)
    cols = width // 128
    slab = cap * cols
    odd = p % 2
    mate = p + 1 - 2 * odd
    other = p - 1 + 2 * odd
    has_mate = mate < doms
    has_other = (other >= 0) & (other < doms)
    mesh_id = pl.DeviceIdType.MESH
    r_i = lax.broadcasted_iota(jnp.int32, (128, 128), 0)
    c_i = lax.broadcasted_iota(jnp.int32, (128, 128), 1)
    steps = [1 << i for i in range(reps.bit_length() - 1)]
    stages = len(steps)

    def flip(step):
        return q + step * (1 - 2 * ((q // step) % 2))

    def signal(sem, dom, rep):
        pl.semaphore_signal(sem, inc=1, device_id={"dom": dom, "rep": rep}, device_id_type=mesh_id)

    def chunk(ch):
        return pl.ds(CH * ch, CH)

    def halo_copy(ch):
        at = chunk(ch)
        return pltpu.make_async_remote_copy(
            src_ref=sbuf.at[:, at], dst_ref=rbuf.at[:, at], send_sem=ssem.at[ch], recv_sem=rsem.at[ch],
            device_id={"dom": mate, "rep": q}, device_id_type=mesh_id)

    def ids_copy():
        return pltpu.make_async_remote_copy(
            src_ref=hblk.at[odd], dst_ref=hob, send_sem=hs, recv_sem=hr,
            device_id={"dom": other, "rep": q}, device_id_type=mesh_id)

    def owner_copy(i):
        at = pl.ds(*parts[i])
        return pltpu.make_async_remote_copy(
            src_ref=G2.at[q, at, :], dst_ref=OG.at[at, :], send_sem=oss.at[i], recv_sem=ors.at[i],
            device_id={"dom": other, "rep": q}, device_id_type=mesh_id)

    def stage(Gx, RBx, ss, rs, number, k):
        slot = 0
        for step in steps[:number]:
            slot += reps // (2 * step)
        step = steps[number]
        bit = (q // step) % 2
        low = q % step
        made = []
        for i in range(reps // (2 * step)):
            away = low + (1 - bit) * step + 2 * step * i
            keep = low + bit * step + 2 * step * i
            at = pl.ds(*parts[k])
            n = (slot + i) * pieces + k
            made.append((pltpu.make_async_remote_copy(
                src_ref=Gx.at[away, at, :], dst_ref=RBx.at[slot + i, at, :],
                send_sem=ss.at[n], recv_sem=rs.at[n],
                device_id={"dom": p, "rep": flip(step)}, device_id_type=mesh_id), keep, slot + i))
        return made

    dsums = (G, RB, xss, xrs)
    osums = (G2, RB2, yss, yrs)

    def stage_start(bufs, number, k):
        for cp, _, _ in stage(*bufs, number, k):
            cp.start()

    def stage_finish(bufs, number, k):
        Gx, RBx = bufs[0], bufs[1]
        at = pl.ds(*parts[k])
        for cp, keep, slot in stage(*bufs, number, k):
            cp.wait_recv()
            Gx[keep, at, :] += RBx[slot, at, :]

    def stage_through(bufs):
        for number in range(stages - 1):
            for k in range(pieces):
                stage_finish(bufs, number, k)
                stage_start(bufs, number + 1, k)

    def stages_done(bufs):
        for number in range(stages):
            for k in range(pieces):
                for cp, _, _ in stage(*bufs, number, k):
                    cp.wait_send()

    barrier = pltpu.get_barrier_semaphore()
    for step in steps:
        signal(barrier, p, flip(step))

    @pl.when(has_mate)
    def _():
        signal(barrier, mate, q)

    @pl.when(has_other)
    def _():
        signal(barrier, other, q)

    for c in range(n_rows // CH):
        TR[:, c * CH : (c + 1) * CH] = rows[c * CH : (c + 1) * CH, :].T

    def pick(ch):
        l = lists[:, pl.ds(pl.multiple_of(((1 - odd) * nch + ch) * CH, CH), CH)]
        i = lax.broadcasted_iota(jnp.int32, (n_rows, CH), 0)
        PT = jnp.where(i == l, 1.0, 0.0).astype(BF)
        sbuf[:, chunk(ch)] = jnp.dot(TR[...], PT, preferred_element_type=F).astype(BF)

    @pl.when(has_mate)
    def _():
        pick(0)

    pl.semaphore_wait(barrier, stages + jnp.where(has_mate, 1, 0) + jnp.where(has_other, 1, 0))

    @pl.when(has_mate)
    def _():
        halo_copy(0).start()

    @pl.when(has_other)
    def _():
        ids_copy().start()

    def meet(i, wait):
        if i >= rounds:
            if wait:
                pl.semaphore_wait(met.at[i - rounds], 1)
            else:
                signal(met.at[i - rounds], p, flip(steps[i - rounds]))
            return
        d = 1 << i
        up, down = p + d < doms, p - d >= 0
        if wait:
            pl.semaphore_wait(near.at[i], jnp.where(up, 1, 0) + jnp.where(down, 1, 0))
            return

        @pl.when(up)
        def _():
            signal(near.at[i], p + d, q)

        @pl.when(down)
        def _():
            signal(near.at[i], p - d, q)

    rounds = (doms - 1).bit_length()
    gone = 0

    def advance():
        nonlocal gone
        if gone > 0:
            meet(gone - 1, True)
        if gone < rounds + stages:
            meet(gone, False)
        gone += 1

    def send(ch):
        @pl.when(has_mate)
        def _():
            pick(ch)
            halo_copy(ch).start()

    advance()
    for ch in range(1, min(2, nch)):
        send(ch)
    advance()

    @pl.when(has_other)
    def _():
        ids_copy().wait_recv()
        half = hob.shape[1]
        l = lists[:, pl.ds(pl.multiple_of(odd * half, half), half)]
        hi, lo = l // 128, l % 128
        i = lax.broadcasted_iota(jnp.int32, (n_rows // 128, half), 0)
        k = lax.broadcasted_iota(jnp.int32, (128, half), 0)
        named = jnp.where(i == hi, (hob[...] + 1).astype(F), 0.0).astype(BF)
        ones = jnp.where(k == lo, 1.0, 0.0).astype(BF)
        ids = lax.dot_general(named, ones, (((1,), (1,)), ((), ())), preferred_element_type=F)
        for c in range(n_rows // 128):
            lids[:, 128 * c : 128 * c + 128] = ids[c : c + 1, :] - 1.0
        gram(G2, TR[...], rows[...], lids[...], False)
        pack_diagonals(G2, r_i, c_i)
        for k in range(pieces):
            stage_start(osums, 0, k)

    @pl.when(jnp.logical_not(has_other))
    def _():
        OG[...] = jnp.zeros_like(OG)

    advance()
    for ch in range(2, nch):
        send(ch)

    n_born = born.shape[0]
    ii = lax.broadcasted_iota(jnp.int32, (n_born, n_born), 0)
    jj = lax.broadcasted_iota(jnp.int32, (n_born, n_born), 1)
    own = jnp.broadcast_to(own_r[...].astype(F), (n_born, n_born))
    same = (own.T == own) & (ii < jj)
    rank = jnp.sum(jnp.where(same, 1.0, 0.0), axis=0, keepdims=True).astype(jnp.int32)
    base = own_r[...] * slab + rank * cols
    m = lax.broadcasted_iota(jnp.int32, (total * slab, n_born), 0)
    acc = jnp.zeros((total * slab, 128), F)
    for c in range(cols):
        oh = jnp.where(m == base + c, 1.0, 0.0).astype(BF)
        acc += jnp.dot(oh, born[:, c * 128 : (c + 1) * 128], preferred_element_type=F)
    bpack[...] = acc.astype(BF)

    @pl.when(has_other)
    def _():
        stage_through(osums)

    advance()
    gram(G, TR[...], rows[...], eblk[...], False)
    while gone <= rounds + stages:
        advance()

    def born_copy(to, frm):
        return pltpu.make_async_remote_copy(
            src_ref=bpack.at[pl.ds(pl.multiple_of(to * slab, slab), slab), :],
            dst_ref=brecv.at[pl.ds(pl.multiple_of(frm * slab, slab), slab), :],
            send_sem=bss.at[to], recv_sem=brs.at[frm],
            device_id={"dom": to // reps, "rep": to % reps}, device_id_type=mesh_id)

    def born_send(k, _):
        to = (me + k) % total
        born_copy(to, me).start()
        return 0

    lax.fori_loop(1, total, born_send, 0)
    mine = pl.ds(pl.multiple_of(me * slab, slab), slab)
    local = pltpu.make_async_copy(bpack.at[mine, :], brecv.at[mine, :], lsem)
    local.start()

    def born_wait(k, _):
        frm = (me + k) % total
        born_copy(frm, frm).wait_recv()
        return 0

    def add_born():
        lax.fori_loop(1, total, born_wait, 0)
        local.wait()
        n = total * cap
        mm = lax.broadcasted_iota(jnp.int32, (n, total * slab), 0)
        kk = lax.broadcasted_iota(jnp.int32, (n, total * slab), 1)
        Bv = brecv[...]
        V = jnp.concatenate(
            [jnp.dot(jnp.where(kk == mm * cols + c, 1.0, 0.0).astype(BF), Bv, preferred_element_type=F)
             for c in range(cols)], axis=1)
        VT = V.T.astype(BF)
        V = V.astype(BF)
        for j in range(cols):
            o = 128 * j
            S[o:, o : o + 128] = scale * jnp.dot(VT[o:, :], V[:, o : o + 128], preferred_element_type=F)
            S[o : o + 128, o : o + 128] += jnp.where(r_i == c_i, mass[:, o : o + 128], 0.0)

    scale = 1.0 / width

    def add_halo(first, last):
        @pl.when(has_mate)
        def _():
            at = pl.ds(CH * first, CH * (last - first))
            T = rbuf[:, at]
            gram(G, T, T.T, hblk[1 - odd, :, at], True)

    def arrive(ch):
        @pl.when(has_mate)
        def _():
            halo_copy(ch).wait_recv()

    @pl.when(has_other)
    def _():
        for k in range(pieces):
            stage_finish(osums, stages - 1, k)

    for ch in range(nch - 1):
        arrive(ch)
    if nch > 1:
        add_halo(0, nch - 1)
    add_born()
    arrive(nch - 1)

    @pl.when(has_other)
    def _():
        for k in range(pieces):
            owner_copy(k).start()

    add_halo(nch - 1, nch)
    pack_diagonals(G, r_i, c_i)
    for k in range(pieces):
        stage_start(dsums, 0, k)
    stage_through(dsums)

    def take(k):
        at = pl.ds(*parts[k])
        (cp, _, slot), = stage(*dsums, stages - 1, k)
        cp.wait_recv()

        @pl.when(has_other)
        def _():
            owner_copy(k).wait_recv()

        def value(first, count):
            at = pl.ds(first, count)
            return scale * (G[q, at, :] + RB[slot, at, :] + OG[at, :])

        def pair(j):
            X = value(diag[j], 128)
            XT = X.T
            ends = DG[j // 2 : j // 2 + 1, :]
            S[128 * j : 128 * j + 128, 128 * j : 128 * j + 128] += jnp.where(c_i <= r_i, X, XT)
            o = 128 * j + 128
            S[o : o + 128, o : o + 128] += jnp.where(c_i > r_i, X, jnp.where(c_i < r_i, XT, ends))

        def column(j):
            o = 128 * j
            S[o + 128 :, o : o + 128] += value(rest[j], width - o - 128)

        if k == 0:
            DG[...] = value(120, 8)
            pair(0)
        elif k % 2 == 0:
            column(k - 1)
            pair(k)
        else:
            column(k - 1)

    def take_to(last):
        nonlocal taken
        while taken <= last:
            take(taken)
            taken += 1

    taken = 0
    for j in range(cols):
        o = 128 * j
        take_to(j - j % 2)
        Ld, W = chol_diag(S[o : o + 128, o : o + 128], A.at[j % 2])
        out[o : o + 128, o : o + 128] = Ld
        m, e = o + 128, o + 256
        if m < width:
            out[o:m, m:] = jnp.zeros((128, width - m), F)
            take_to(j + 1)
            near_rows = dot_t(S[m:e, o:m], W)
            S[m:e, m:e] = S[m:e, m:e] - dot_t(near_rows, near_rows)
            out[m:e, o:m] = near_rows
        if e < width:
            far_rows = dot_t(S[e:, o:m], W)
            out[e:, o:m] = far_rows
            S[e:, m:e] = S[e:, m:e] - dot_t(far_rows, near_rows)
            for c in range(e, width, 128):
                S[c:, c : c + 128] = S[c:, c : c + 128] - dot_t(far_rows[c - e :], far_rows[c - e : c - e + 128])

    stages_done(dsums)

    @pl.when(has_other)
    def _():
        ids_copy().wait_send()
        stages_done(osums)
        for k in range(pieces):
            owner_copy(k).wait_send()

    def born_done(k, _):
        to = (me + k) % total
        born_copy(to, me).wait_send()
        return 0

    lax.fori_loop(1, total, born_done, 0)

    @pl.when(has_mate)
    def _():
        for ch in range(nch):
            halo_copy(ch).wait_send()


def solution(mesh):
    doms, reps = mesh.shape["dom"], mesh.shape["rep"]
    total = doms * reps

    def local(elem_rows, elem_block, send_lists, halo_block, born_rows, born_owner, mass):
        n_rows, width = elem_rows.shape
        half = send_lists.shape[0] // 2
        nch = half // CH
        _, _, parts, tri = layout(width)
        pieces = len(parts)
        slab = CAP * (width // 128)
        rounds = max(1, (doms - 1).bit_length())
        stages = max(1, reps.bit_length() - 1)
        dma = pltpu.SemaphoreType.DMA
        vm = pl.BlockSpec(memory_space=pltpu.VMEM)
        return pl.pallas_call(
            functools.partial(exchange_kernel, doms, reps, CAP),
            out_shape=jax.ShapeDtypeStruct((width, width), F),
            in_specs=[vm] * 7,
            out_specs=vm,
            scratch_shapes=[
                pltpu.VMEM((width, width), F),
                pltpu.VMEM((2, 128, 256), F),
                pltpu.VMEM((8, 128), F),
                pltpu.VMEM((width, n_rows), BF),
                pltpu.VMEM((width, half), BF),
                pltpu.VMEM((width, half), BF),
                pltpu.VMEM((1, n_rows), F),
                pltpu.VMEM((1, half), jnp.int32),
                pltpu.VMEM((reps, tri, 128), F),
                pltpu.VMEM((reps - 1, tri, 128), F),
                pltpu.VMEM((reps, tri, 128), F),
                pltpu.VMEM((reps - 1, tri, 128), F),
                pltpu.VMEM((tri, 128), F),
                pltpu.VMEM((total * slab, 128), BF),
                pltpu.VMEM((total * slab, 128), BF),
                dma((nch,)),
                dma((nch,)),
                dma,
                dma,
                dma((total,)),
                dma((total,)),
                dma(((reps - 1) * pieces,)),
                dma(((reps - 1) * pieces,)),
                dma(((reps - 1) * pieces,)),
                dma(((reps - 1) * pieces,)),
                dma((pieces,)),
                dma((pieces,)),
                dma,
                pltpu.SemaphoreType.REGULAR((rounds,)),
                pltpu.SemaphoreType.REGULAR((stages,)),
            ],
            compiler_params=pltpu.CompilerParams(
                collective_id=0, has_side_effects=True, vmem_limit_bytes=63 * 1024 * 1024),
        )(elem_rows, elem_block[None, :], send_lists[None, :], halo_block.reshape(2, 1, half),
          born_rows, born_owner.reshape(1, -1), mass[None, :])

    both = P(("dom", "rep"))
    rows2 = P(("dom", "rep"), None)
    return jax.shard_map(local, mesh=mesh, in_specs=(rows2, both, both, both, rows2, rows2, both),
                         out_specs=rows2, check_vma=False)
```

```python
import functools

import jax
import jax.numpy as jnp
from jax import lax
from jax.experimental import pallas as pl
from jax.experimental.pallas import tpu as pltpu
from jax.sharding import PartitionSpec as P

CAP = 4
F=jnp.float32; BF=jnp.bfloat16

def split3(v):
    hi=v.astype(BF); r=v-hi.astype(F); mid=r.astype(BF); lo=(r-mid.astype(F)).astype(BF)
    return hi,mid,lo

def chol_diag(D, A, inverse=True):
    nb=D.shape[0]; st=16
    r_i=lax.broadcasted_iota(jnp.int32,(nb,nb),0); c_i=lax.broadcasted_iota(jnp.int32,(nb,nb),1)
    A[:, :nb]=D
    if inverse:
        A[:, nb:]=jnp.where(r_i==c_i,1.0,0.0)
    wide=2*nb if inverse else nb
    sub=lax.broadcasted_iota(jnp.int32,(st,nb),0)
    T=[A[0:st,h:h+nb] for h in range(0,wide,nb)]
    for s in range(nb//st):
        a=s*st
        B=[jnp.broadcast_to(T[0][:,a+c:a+c+1],(st,nb)) for c in range(st)]
        D=jnp.zeros((st,nb),F)
        for c in range(st):
            piv=jnp.broadcast_to(B[c][c:c+1,:],(st,nb))
            D=jnp.where(sub==c,piv,D)
            if c<st-1:
                m=jnp.where(sub>c,B[c]/piv,0.0)
                for e in range(c+1,st):
                    B[e]=B[e]-m*B[e][c:c+1,:]
                T=[x-m*x[c:c+1,:] for x in T]
        q=lax.rsqrt(D)
        V=jnp.concatenate([x*q for x in T],axis=1)
        A[a:a+st,:wide]=V
        if s<nb//st-1:
            hi,mid,lo=split3(V)
            L=jnp.concatenate([hi,hi,mid,hi,mid,lo],axis=0)[:,:nb].T
            R=jnp.concatenate([hi,mid,hi,lo,mid,hi],axis=0)
            b=a+st; e=b+st
            N=A[b:e,:wide]-jnp.dot(L[b:e],R,preferred_element_type=F)
            T=[N[:,h:h+nb] for h in range(0,wide,nb)]
            if e<nb:
                A[e:,:wide]=A[e:,:wide]-jnp.dot(L[e:],R,preferred_element_type=F)
    Ld=jnp.where(c_i<=r_i,A[:,:nb].T,0.0)
    return (Ld, jnp.where(c_i<=r_i,A[:,nb:],0.0)) if inverse else Ld


def dot_t(x, y):
    xh, xm, xl = split3(x)
    yh, ym, yl = split3(y)
    return lax.dot_general(jnp.concatenate([xh, xh, xm, xh, xm, xl], axis=1),
                           jnp.concatenate([yh, ym, yh, yl, ym, yh], axis=1),
                           (((1,), (1,)), ((), ())), preferred_element_type=F)


CH = 256


def layout(width):
    cols = width // 128
    diag, rest, parts, at = {1: 0, 0: 128}, {0: 256}, [(120, 136), (256, width - 128)], 128 + width
    for j in range(2, cols, 2):
        rest[j - 1], diag[j] = at, at + width - 128 * j
        parts.append((at, width - 128 * (j - 1)))
        at += width - 128 * (j - 1)
        rest[j] = at
        parts.append((at, width - 128 * (j + 1)))
        at += width - 128 * (j + 1)
    rest[cols - 1] = at
    for j in range(3, cols, 2):
        diag[j] = at
        at += 128
    return diag, rest, parts, at


def gram(G, T, R, ids, add):
    reps, width = G.shape[0], R.shape[1]
    diag, rest, _, _ = layout(width)
    M = [jnp.where(ids == b, T, jnp.zeros((), T.dtype)) for b in range(reps)]

    def put(b, first, y):
        at = pl.ds(first, y.shape[0])
        if add:
            G[b, at, :] += y
        else:
            G[b, at, :] = y

    for j in range(0, width // 128, 2):
        o = 128 * j
        h = width - o
        p = jnp.dot(jnp.concatenate([x[o:, :] for x in M], axis=0), R[:, o : o + 256],
                    preferred_element_type=F)
        for b in range(reps):
            y = p[b * h : (b + 1) * h, :]
            put(b, diag[j], y[:128, :128])
            put(b, rest[j], y[128:, :128])
            put(b, diag[j + 1], y[128:256, 128:])
            if h > 256:
                put(b, rest[j + 1], y[256:, 128:])


def pack_diagonals(G, r_i, c_i):
    width = 128
    cols = 1
    while layout_rows(cols) < G.shape[1]:
        cols += 1
    diag, _, _, _ = layout(width * cols)
    for b in range(G.shape[0]):
        ends = []
        for j in range(0, cols, 2):
            low, up = slice(diag[j], diag[j] + 128), slice(diag[j + 1], diag[j + 1] + 128)
            Y = G[b, up, :]
            ends.append(jnp.sum(jnp.where(r_i == c_i, Y, 0.0), axis=0, keepdims=True))
            G[b, low, :] = jnp.where(c_i <= r_i, G[b, low, :], Y)
        pad = jnp.zeros((8 - len(ends), 128), F)
        G[b, 120:128, :] = jnp.concatenate(ends + [pad], axis=0)


def layout_rows(cols):
    return cols * (cols + 1) // 2 * 128


def exchange_kernel(doms, reps, cap, rows, eblk, lists, hblk, born, own_r, mass, out, tail,
                    S, A, LO, DG, TR, sbuf, rbuf, lids, hob, G, RB, G2, RB2, OG, bpack, brecv,
                    ssem, rsem, hs, hr, bss, brs, xss, xrs, yss, yrs, oss, ors, lsem, near, met, fsem):
    p = lax.axis_index("dom")
    q = lax.axis_index("rep")
    me = p * reps + q
    total = doms * reps
    n_rows, width = rows.shape
    nch = ssem.shape[0]
    diag, rest, parts, _ = layout(width)
    pieces = len(parts)
    cols = width // 128
    slab = cap * cols
    odd = p % 2
    mate = p + 1 - 2 * odd
    other = p - 1 + 2 * odd
    has_mate = mate < doms
    has_other = (other >= 0) & (other < doms)
    mesh_id = pl.DeviceIdType.MESH
    r_i = lax.broadcasted_iota(jnp.int32, (128, 128), 0)
    c_i = lax.broadcasted_iota(jnp.int32, (128, 128), 1)
    steps = [1 << i for i in range(reps.bit_length() - 1)]
    stages = len(steps)

    def flip(step):
        return q + step * (1 - 2 * ((q // step) % 2))

    def signal(sem, dom, rep):
        pl.semaphore_signal(sem, inc=1, device_id={"dom": dom, "rep": rep}, device_id_type=mesh_id)

    def chunk(ch):
        return pl.ds(CH * ch, CH)

    def halo_copy(ch):
        at = chunk(ch)
        return pltpu.make_async_remote_copy(
            src_ref=sbuf.at[:, at], dst_ref=rbuf.at[:, at], send_sem=ssem.at[ch], recv_sem=rsem.at[ch],
            device_id={"dom": mate, "rep": q}, device_id_type=mesh_id)

    def ids_copy():
        return pltpu.make_async_remote_copy(
            src_ref=hblk.at[odd], dst_ref=hob, send_sem=hs, recv_sem=hr,
            device_id={"dom": other, "rep": q}, device_id_type=mesh_id)

    def owner_copy(i):
        at = pl.ds(*parts[i])
        return pltpu.make_async_remote_copy(
            src_ref=G2.at[q, at, :], dst_ref=OG.at[at, :], send_sem=oss.at[i], recv_sem=ors.at[i],
            device_id={"dom": other, "rep": q}, device_id_type=mesh_id)

    def stage(Gx, RBx, ss, rs, number, k):
        slot = 0
        for step in steps[:number]:
            slot += reps // (2 * step)
        step = steps[number]
        bit = (q // step) % 2
        low = q % step
        made = []
        for i in range(reps // (2 * step)):
            away = low + (1 - bit) * step + 2 * step * i
            keep = low + bit * step + 2 * step * i
            at = pl.ds(*parts[k])
            n = (slot + i) * pieces + k
            made.append((pltpu.make_async_remote_copy(
                src_ref=Gx.at[away, at, :], dst_ref=RBx.at[slot + i, at, :],
                send_sem=ss.at[n], recv_sem=rs.at[n],
                device_id={"dom": p, "rep": flip(step)}, device_id_type=mesh_id), keep, slot + i))
        return made

    dsums = (G, RB, xss, xrs)
    osums = (G2, RB2, yss, yrs)

    def stage_start(bufs, number, k):
        for cp, _, _ in stage(*bufs, number, k):
            cp.start()

    def stage_finish(bufs, number, k):
        Gx, RBx = bufs[0], bufs[1]
        at = pl.ds(*parts[k])
        for cp, keep, slot in stage(*bufs, number, k):
            cp.wait_recv()
            Gx[keep, at, :] += RBx[slot, at, :]

    def stage_through(bufs):
        for number in range(stages - 1):
            for k in range(pieces):
                stage_finish(bufs, number, k)
                stage_start(bufs, number + 1, k)

    def stages_done(bufs):
        for number in range(stages):
            for k in range(pieces):
                for cp, _, _ in stage(*bufs, number, k):
                    cp.wait_send()

    barrier = pltpu.get_barrier_semaphore()
    for step in steps:
        signal(barrier, p, flip(step))

    @pl.when(has_mate)
    def _():
        signal(barrier, mate, q)

    @pl.when(has_other)
    def _():
        signal(barrier, other, q)

    for c in range(n_rows // CH):
        TR[:, c * CH : (c + 1) * CH] = rows[c * CH : (c + 1) * CH, :].T

    def pick(ch):
        l = lists[:, pl.ds(pl.multiple_of(((1 - odd) * nch + ch) * CH, CH), CH)]
        i = lax.broadcasted_iota(jnp.int32, (n_rows, CH), 0)
        PT = jnp.where(i == l, 1.0, 0.0).astype(BF)
        sbuf[:, chunk(ch)] = jnp.dot(TR[...], PT, preferred_element_type=F).astype(BF)

    @pl.when(has_mate)
    def _():
        pick(0)

    pl.semaphore_wait(barrier, stages + jnp.where(has_mate, 1, 0) + jnp.where(has_other, 1, 0))

    @pl.when(has_mate)
    def _():
        halo_copy(0).start()

    @pl.when(has_other)
    def _():
        ids_copy().start()

    def meet(i, wait):
        if i >= rounds:
            if wait:
                pl.semaphore_wait(met.at[i - rounds], 1)
            else:
                signal(met.at[i - rounds], p, flip(steps[i - rounds]))
            return
        d = 1 << i
        up, down = p + d < doms, p - d >= 0
        if wait:
            pl.semaphore_wait(near.at[i], jnp.where(up, 1, 0) + jnp.where(down, 1, 0))
            return

        @pl.when(up)
        def _():
            signal(near.at[i], p + d, q)

        @pl.when(down)
        def _():
            signal(near.at[i], p - d, q)

    rounds = (doms - 1).bit_length()
    gone = 0

    def advance():
        nonlocal gone
        if gone > 0:
            meet(gone - 1, True)
        if gone < rounds + stages:
            meet(gone, False)
        gone += 1

    def send(ch):
        @pl.when(has_mate)
        def _():
            pick(ch)
            halo_copy(ch).start()

    advance()
    for ch in range(1, min(2, nch)):
        send(ch)
    advance()

    @pl.when(has_other)
    def _():
        ids_copy().wait_recv()
        half = hob.shape[1]
        l = lists[:, pl.ds(pl.multiple_of(odd * half, half), half)]
        hi, lo = l // 128, l % 128
        i = lax.broadcasted_iota(jnp.int32, (n_rows // 128, half), 0)
        k = lax.broadcasted_iota(jnp.int32, (128, half), 0)
        named = jnp.where(i == hi, (hob[...] + 1).astype(F), 0.0).astype(BF)
        ones = jnp.where(k == lo, 1.0, 0.0).astype(BF)
        ids = lax.dot_general(named, ones, (((1,), (1,)), ((), ())), preferred_element_type=F)
        for c in range(n_rows // 128):
            lids[:, 128 * c : 128 * c + 128] = ids[c : c + 1, :] - 1.0
        gram(G2, TR[...], rows[...], lids[...], False)
        pack_diagonals(G2, r_i, c_i)
        for k in range(pieces):
            stage_start(osums, 0, k)

    @pl.when(jnp.logical_not(has_other))
    def _():
        OG[...] = jnp.zeros_like(OG)

    advance()
    for ch in range(2, nch):
        send(ch)

    n_born = born.shape[0]
    ii = lax.broadcasted_iota(jnp.int32, (n_born, n_born), 0)
    jj = lax.broadcasted_iota(jnp.int32, (n_born, n_born), 1)
    own = jnp.broadcast_to(own_r[...].astype(F), (n_born, n_born))
    same = (own.T == own) & (ii < jj)
    rank = jnp.sum(jnp.where(same, 1.0, 0.0), axis=0, keepdims=True).astype(jnp.int32)
    base = own_r[...] * slab + rank * cols
    m = lax.broadcasted_iota(jnp.int32, (total * slab, n_born), 0)
    acc = jnp.zeros((total * slab, 128), F)
    for c in range(cols):
        oh = jnp.where(m == base + c, 1.0, 0.0).astype(BF)
        acc += jnp.dot(oh, born[:, c * 128 : (c + 1) * 128], preferred_element_type=F)
    bpack[...] = acc.astype(BF)

    @pl.when(has_other)
    def _():
        stage_through(osums)

    while gone <= rounds + stages:
        advance()

    def born_copy(to, frm):
        return pltpu.make_async_remote_copy(
            src_ref=bpack.at[pl.ds(pl.multiple_of(to * slab, slab), slab), :],
            dst_ref=brecv.at[pl.ds(pl.multiple_of(frm * slab, slab), slab), :],
            send_sem=bss.at[to], recv_sem=brs.at[frm],
            device_id={"dom": to // reps, "rep": to % reps}, device_id_type=mesh_id)

    def born_send(k, _):
        to = (me + k) % total
        born_copy(to, me).start()
        return 0

    lax.fori_loop(1, total, born_send, 0)
    mine = pl.ds(pl.multiple_of(me * slab, slab), slab)
    local = pltpu.make_async_copy(bpack.at[mine, :], brecv.at[mine, :], lsem)
    local.start()

    gram(G, TR[...], rows[...], eblk[...], False)

    def born_wait(k, _):
        frm = (me + k) % total
        born_copy(frm, frm).wait_recv()
        return 0

    def add_born():
        lax.fori_loop(1, total, born_wait, 0)
        local.wait()
        n = total * cap
        mm = lax.broadcasted_iota(jnp.int32, (n, total * slab), 0)
        kk = lax.broadcasted_iota(jnp.int32, (n, total * slab), 1)
        Bv = brecv[...]
        V = jnp.concatenate(
            [jnp.dot(jnp.where(kk == mm * cols + c, 1.0, 0.0).astype(BF), Bv, preferred_element_type=F)
             for c in range(cols)], axis=1)
        VT = V.T.astype(BF)
        V = V.astype(BF)
        for j in range(cols):
            o = 128 * j
            S[o:, o : o + 128] = scale * jnp.dot(VT[o:, :], V[:, o : o + 128], preferred_element_type=F)
            S[o : o + 128, o : o + 128] += jnp.where(r_i == c_i, mass[:, o : o + 128], 0.0)

    scale = 1.0 / width

    def add_halo(first, last):
        @pl.when(has_mate)
        def _():
            at = pl.ds(CH * first, CH * (last - first))
            T = rbuf[:, at]
            gram(G, T, T.T, hblk[1 - odd, :, at], True)

    def arrive(ch):
        @pl.when(has_mate)
        def _():
            halo_copy(ch).wait_recv()

    @pl.when(has_other)
    def _():
        for k in range(pieces):
            stage_finish(osums, stages - 1, k)

    for ch in range(nch - 1):
        arrive(ch)
    if nch > 1:
        add_halo(0, nch - 1)
    arrive(nch - 1)

    add_halo(nch - 1, nch)
    pack_diagonals(G, r_i, c_i)
    for k in range(pieces):
        stage_start(dsums, 0, k)
    add_born()

    @pl.when(has_other)
    def _():
        for k in range(pieces):
            owner_copy(k).start()

    stage_through(dsums)

    def take(k):
        at = pl.ds(*parts[k])
        (cp, _, slot), = stage(*dsums, stages - 1, k)
        cp.wait_recv()

        @pl.when(has_other)
        def _():
            owner_copy(k).wait_recv()

        def value(first, count):
            at = pl.ds(first, count)
            return scale * (G[q, at, :] + RB[slot, at, :] + OG[at, :])

        def pair(j):
            X = value(diag[j], 128)
            XT = X.T
            ends = DG[j // 2 : j // 2 + 1, :]
            S[128 * j : 128 * j + 128, 128 * j : 128 * j + 128] += jnp.where(c_i <= r_i, X, XT)
            o = 128 * j + 128
            S[o : o + 128, o : o + 128] += jnp.where(c_i > r_i, X, jnp.where(c_i < r_i, XT, ends))

        def column(j):
            o = 128 * j
            S[o + 128 :, o : o + 128] += value(rest[j], width - o - 128)

        if k == 0:
            DG[...] = value(120, 8)
            pair(0)
        elif k % 2 == 0:
            column(k - 1)
            pair(k)
        else:
            column(k - 1)

    def take_to(last):
        nonlocal taken
        while taken <= last:
            take(taken)
            taken += 1

    def leave(j):
        at = pl.ds(128 * j, 128)
        return pltpu.make_async_copy(LO.at[:, at], out.at[:, at], fsem.at[j])

    taken = 0
    for j in range(cols - 1):
        o, m, e = 128 * j, 128 * j + 128, 128 * j + 256
        take_to(j - j % 2)
        Ld, W = chol_diag(S[o:m, o:m], A.at[j % 2])
        LO[o:m, o:m] = Ld
        if j:
            LO[:o, o:m] = jnp.zeros((o, 128), F)
        take_to(j + 1)
        near_rows = dot_t(S[m:e, o:m], W)
        S[m:e, m:e] = S[m:e, m:e] - dot_t(near_rows, near_rows)
        LO[m:e, o:m] = near_rows
        if e < width:
            far_rows = dot_t(S[e:, o:m], W)
            LO[e:, o:m] = far_rows
            S[e:, m:e] = S[e:, m:e] - dot_t(far_rows, near_rows)
            for c in range(e, width, 128):
                S[c:, c : c + 128] = S[c:, c : c + 128] - dot_t(far_rows[c - e :], far_rows[c - e : c - e + 128])
        leave(j).start()
    tail[...] = S[width - 128 :, width - 128 :]

    stages_done(dsums)

    @pl.when(has_other)
    def _():
        ids_copy().wait_send()
        stages_done(osums)
        for k in range(pieces):
            owner_copy(k).wait_send()

    def born_done(k, _):
        to = (me + k) % total
        born_copy(to, me).wait_send()
        return 0

    lax.fori_loop(1, total, born_done, 0)

    @pl.when(has_mate)
    def _():
        for ch in range(nch):
            halo_copy(ch).wait_send()


    for j in range(cols - 1):
        leave(j).wait()


def finish_kernel(L, D, out, A):
    width = out.shape[0]
    cut = width - 128
    out[:, :cut] = L[...]
    out[:cut, cut:] = jnp.zeros((cut, 128), F)
    out[cut:, cut:] = chol_diag(D[...], A, inverse=False)


def solution(mesh):
    doms, reps = mesh.shape["dom"], mesh.shape["rep"]
    total = doms * reps

    def local(elem_rows, elem_block, send_lists, halo_block, born_rows, born_owner, mass):
        n_rows, width = elem_rows.shape
        half = send_lists.shape[0] // 2
        nch = half // CH
        _, _, parts, tri = layout(width)
        pieces = len(parts)
        slab = CAP * (width // 128)
        rounds = max(1, (doms - 1).bit_length())
        stages = max(1, reps.bit_length() - 1)
        dma = pltpu.SemaphoreType.DMA
        vm = pl.BlockSpec(memory_space=pltpu.VMEM)
        far = pl.BlockSpec(memory_space=pl.ANY)
        L, D = pl.pallas_call(
            functools.partial(exchange_kernel, doms, reps, CAP),
            out_shape=(jax.ShapeDtypeStruct((width, width - 128), F), jax.ShapeDtypeStruct((128, 128), F)),
            in_specs=[vm] * 7,
            out_specs=(far, vm),
            scratch_shapes=[
                pltpu.VMEM((width, width), F),
                pltpu.VMEM((2, 128, 256), F),
                pltpu.VMEM((width, width - 128), F),
                pltpu.VMEM((8, 128), F),
                pltpu.VMEM((width, n_rows), BF),
                pltpu.VMEM((width, half), BF),
                pltpu.VMEM((width, half), BF),
                pltpu.VMEM((1, n_rows), F),
                pltpu.VMEM((1, half), jnp.int32),
                pltpu.VMEM((reps, tri, 128), F),
                pltpu.VMEM((reps - 1, tri, 128), F),
                pltpu.VMEM((reps, tri, 128), F),
                pltpu.VMEM((reps - 1, tri, 128), F),
                pltpu.VMEM((tri, 128), F),
                pltpu.VMEM((total * slab, 128), BF),
                pltpu.VMEM((total * slab, 128), BF),
                dma((nch,)),
                dma((nch,)),
                dma,
                dma,
                dma((total,)),
                dma((total,)),
                dma(((reps - 1) * pieces,)),
                dma(((reps - 1) * pieces,)),
                dma(((reps - 1) * pieces,)),
                dma(((reps - 1) * pieces,)),
                dma((pieces,)),
                dma((pieces,)),
                dma,
                pltpu.SemaphoreType.REGULAR((rounds,)),
                pltpu.SemaphoreType.REGULAR((stages,)),
                dma((width // 128 - 1,)),
            ],
            compiler_params=pltpu.CompilerParams(
                collective_id=0, has_side_effects=True, vmem_limit_bytes=63 * 1024 * 1024),
        )(elem_rows, elem_block[None, :], send_lists[None, :], halo_block.reshape(2, 1, half),
          born_rows, born_owner.reshape(1, -1), mass[None, :])
        return pl.pallas_call(
            finish_kernel,
            out_shape=jax.ShapeDtypeStruct((width, width), F),
            in_specs=[vm, vm],
            out_specs=vm,
            scratch_shapes=[pltpu.VMEM((128, 128), F)],
        )(L, D)

    both = P(("dom", "rep"))
    rows2 = P(("dom", "rep"), None)
    return jax.shard_map(local, mesh=mesh, in_specs=(rows2, both, both, both, rows2, rows2, both),
                         out_specs=rows2, check_vma=False)
```

```python
import functools

import jax
import jax.numpy as jnp
from jax import lax
from jax.experimental import pallas as pl
from jax.experimental.pallas import tpu as pltpu
from jax.sharding import PartitionSpec as P

CAP = 4
F=jnp.float32; BF=jnp.bfloat16

def split3(v):
    hi=v.astype(BF); r=v-hi.astype(F); mid=r.astype(BF); lo=(r-mid.astype(F)).astype(BF)
    return hi,mid,lo

def chol_diag(D, A, inverse=True):
    nb=D.shape[0]; st=16
    r_i=lax.broadcasted_iota(jnp.int32,(nb,nb),0); c_i=lax.broadcasted_iota(jnp.int32,(nb,nb),1)
    A[:, :nb]=D
    if inverse:
        A[:, nb:]=jnp.where(r_i==c_i,1.0,0.0)
    wide=2*nb if inverse else nb
    sub=lax.broadcasted_iota(jnp.int32,(st,nb),0)
    T=[A[0:st,h:h+nb] for h in range(0,wide,nb)]
    for s in range(nb//st):
        a=s*st
        B=[jnp.broadcast_to(T[0][:,a+c:a+c+1],(st,nb)) for c in range(st)]
        D=jnp.zeros((st,nb),F)
        for c in range(st):
            piv=jnp.broadcast_to(B[c][c:c+1,:],(st,nb))
            D=jnp.where(sub==c,piv,D)
            if c<st-1:
                m=jnp.where(sub>c,B[c]/piv,0.0)
                for e in range(c+1,st):
                    B[e]=B[e]-m*B[e][c:c+1,:]
                T=[x-m*x[c:c+1,:] for x in T]
        q=lax.rsqrt(D)
        V=jnp.concatenate([x*q for x in T],axis=1)
        A[a:a+st,:wide]=V
        if s<nb//st-1:
            hi,mid,lo=split3(V)
            L=jnp.concatenate([hi,hi,mid,hi,mid,lo],axis=0)[:,:nb].T
            R=jnp.concatenate([hi,mid,hi,lo,mid,hi],axis=0)
            b=a+st; e=b+st
            N=A[b:e,:wide]-jnp.dot(L[b:e],R,preferred_element_type=F)
            T=[N[:,h:h+nb] for h in range(0,wide,nb)]
            if e<nb:
                A[e:,:wide]=A[e:,:wide]-jnp.dot(L[e:],R,preferred_element_type=F)
    Ld=jnp.where(c_i<=r_i,A[:,:nb].T,0.0)
    return (Ld, jnp.where(c_i<=r_i,A[:,nb:],0.0)) if inverse else Ld


def dot_t(x, y):
    xh, xm, xl = split3(x)
    yh, ym, yl = split3(y)
    return lax.dot_general(jnp.concatenate([xh, xh, xm, xh, xm, xl], axis=1),
                           jnp.concatenate([yh, ym, yh, yl, ym, yh], axis=1),
                           (((1,), (1,)), ((), ())), preferred_element_type=F)


CH = 256


def layout(width):
    cols = width // 128
    diag, rest, parts, at = {1: 0, 0: 128}, {0: 256}, [(120, 136), (256, width - 128)], 128 + width
    for j in range(2, cols, 2):
        rest[j - 1], diag[j] = at, at + width - 128 * j
        parts.append((at, width - 128 * (j - 1)))
        at += width - 128 * (j - 1)
        rest[j] = at
        parts.append((at, width - 128 * (j + 1)))
        at += width - 128 * (j + 1)
    rest[cols - 1] = at
    for j in range(3, cols, 2):
        diag[j] = at
        at += 128
    return diag, rest, parts, at


def gram(G, T, R, ids, add):
    reps, width = G.shape[0], R.shape[1]
    diag, rest, _, _ = layout(width)
    M = [jnp.where(ids == b, T, jnp.zeros((), T.dtype)) for b in range(reps)]

    def put(b, first, y):
        at = pl.ds(first, y.shape[0])
        if add:
            G[b, at, :] += y
        else:
            G[b, at, :] = y

    for j in range(0, width // 128, 2):
        o = 128 * j
        h = width - o
        p = jnp.dot(jnp.concatenate([x[o:, :] for x in M], axis=0), R[:, o : o + 256],
                    preferred_element_type=F)
        for b in range(reps):
            y = p[b * h : (b + 1) * h, :]
            put(b, diag[j], y[:128, :128])
            put(b, rest[j], y[128:, :128])
            put(b, diag[j + 1], y[128:256, 128:])
            if h > 256:
                put(b, rest[j + 1], y[256:, 128:])


def pack_diagonals(G, r_i, c_i):
    width = 128
    cols = 1
    while layout_rows(cols) < G.shape[1]:
        cols += 1
    diag, _, _, _ = layout(width * cols)
    for b in range(G.shape[0]):
        ends = []
        for j in range(0, cols, 2):
            low, up = slice(diag[j], diag[j] + 128), slice(diag[j + 1], diag[j + 1] + 128)
            Y = G[b, up, :]
            ends.append(jnp.sum(jnp.where(r_i == c_i, Y, 0.0), axis=0, keepdims=True))
            G[b, low, :] = jnp.where(c_i <= r_i, G[b, low, :], Y)
        pad = jnp.zeros((8 - len(ends), 128), F)
        G[b, 120:128, :] = jnp.concatenate(ends + [pad], axis=0)


def layout_rows(cols):
    return cols * (cols + 1) // 2 * 128


def exchange_kernel(doms, reps, cap, rows, eblk, lists, hblk, born, own_r, mass, out, tail,
                    S, A, LO, DG, TR, sbuf, rbuf, lids, hob, G, RB, G2, RB2, OG, bpack, brecv,
                    ssem, rsem, hs, hr, bss, brs, xss, xrs, yss, yrs, oss, ors, lsem, near, met, fsem):
    p = lax.axis_index("dom")
    q = lax.axis_index("rep")
    me = p * reps + q
    total = doms * reps
    n_rows, width = rows.shape
    nch = ssem.shape[0]
    diag, rest, parts, _ = layout(width)
    pieces = len(parts)
    cols = width // 128
    slab = cap * cols
    odd = p % 2
    mate = p + 1 - 2 * odd
    other = p - 1 + 2 * odd
    has_mate = mate < doms
    has_other = (other >= 0) & (other < doms)
    mesh_id = pl.DeviceIdType.MESH
    r_i = lax.broadcasted_iota(jnp.int32, (128, 128), 0)
    c_i = lax.broadcasted_iota(jnp.int32, (128, 128), 1)
    steps = [1 << i for i in range(reps.bit_length() - 1)]
    stages = len(steps)

    def flip(step):
        return q + step * (1 - 2 * ((q // step) % 2))

    def signal(sem, dom, rep):
        pl.semaphore_signal(sem, inc=1, device_id={"dom": dom, "rep": rep}, device_id_type=mesh_id)

    def chunk(ch):
        return pl.ds(CH * ch, CH)

    def halo_copy(ch):
        at = chunk(ch)
        return pltpu.make_async_remote_copy(
            src_ref=sbuf.at[:, at], dst_ref=rbuf.at[:, at], send_sem=ssem.at[ch], recv_sem=rsem.at[ch],
            device_id={"dom": mate, "rep": q}, device_id_type=mesh_id)

    def ids_copy():
        return pltpu.make_async_remote_copy(
            src_ref=hblk.at[odd], dst_ref=hob, send_sem=hs, recv_sem=hr,
            device_id={"dom": other, "rep": q}, device_id_type=mesh_id)

    def owner_copy(i):
        at = pl.ds(*parts[i])
        return pltpu.make_async_remote_copy(
            src_ref=G2.at[q, at, :], dst_ref=OG.at[at, :], send_sem=oss.at[i], recv_sem=ors.at[i],
            device_id={"dom": other, "rep": q}, device_id_type=mesh_id)

    def stage(Gx, RBx, ss, rs, number, k):
        slot = 0
        for step in steps[:number]:
            slot += reps // (2 * step)
        step = steps[number]
        bit = (q // step) % 2
        low = q % step
        made = []
        for i in range(reps // (2 * step)):
            away = low + (1 - bit) * step + 2 * step * i
            keep = low + bit * step + 2 * step * i
            at = pl.ds(*parts[k])
            n = (slot + i) * pieces + k
            made.append((pltpu.make_async_remote_copy(
                src_ref=Gx.at[away, at, :], dst_ref=RBx.at[slot + i, at, :],
                send_sem=ss.at[n], recv_sem=rs.at[n],
                device_id={"dom": p, "rep": flip(step)}, device_id_type=mesh_id), keep, slot + i))
        return made

    dsums = (G, RB, xss, xrs)
    osums = (G2, RB2, yss, yrs)

    def stage_start(bufs, number, k):
        for cp, _, _ in stage(*bufs, number, k):
            cp.start()

    def stage_finish(bufs, number, k):
        Gx, RBx = bufs[0], bufs[1]
        at = pl.ds(*parts[k])
        for cp, keep, slot in stage(*bufs, number, k):
            cp.wait_recv()
            Gx[keep, at, :] += RBx[slot, at, :]

    def stage_through(bufs, ks):
        for number in range(stages - 1):
            for k in ks:
                stage_finish(bufs, number, k)
                stage_start(bufs, number + 1, k)

    def stages_done(bufs):
        for number in range(stages):
            for k in range(pieces):
                for cp, _, _ in stage(*bufs, number, k):
                    cp.wait_send()

    barrier = pltpu.get_barrier_semaphore()
    for step in steps:
        signal(barrier, p, flip(step))

    @pl.when(has_mate)
    def _():
        signal(barrier, mate, q)

    @pl.when(has_other)
    def _():
        signal(barrier, other, q)

    for c in range(n_rows // CH):
        TR[:, c * CH : (c + 1) * CH] = rows[c * CH : (c + 1) * CH, :].T

    def pick(ch):
        l = lists[:, pl.ds(pl.multiple_of(((1 - odd) * nch + ch) * CH, CH), CH)]
        i = lax.broadcasted_iota(jnp.int32, (n_rows, CH), 0)
        PT = jnp.where(i == l, 1.0, 0.0).astype(BF)
        sbuf[:, chunk(ch)] = jnp.dot(TR[...], PT, preferred_element_type=F).astype(BF)

    @pl.when(has_mate)
    def _():
        pick(0)

    pl.semaphore_wait(barrier, stages + jnp.where(has_mate, 1, 0) + jnp.where(has_other, 1, 0))

    @pl.when(has_mate)
    def _():
        halo_copy(0).start()

    @pl.when(has_other)
    def _():
        ids_copy().start()

    def meet(i, wait):
        if i >= rounds:
            if wait:
                pl.semaphore_wait(met.at[i - rounds], 1)
            else:
                signal(met.at[i - rounds], p, flip(steps[i - rounds]))
            return
        d = 1 << i
        up, down = p + d < doms, p - d >= 0
        if wait:
            pl.semaphore_wait(near.at[i], jnp.where(up, 1, 0) + jnp.where(down, 1, 0))
            return

        @pl.when(up)
        def _():
            signal(near.at[i], p + d, q)

        @pl.when(down)
        def _():
            signal(near.at[i], p - d, q)

    rounds = (doms - 1).bit_length()
    gone = 0

    def advance():
        nonlocal gone
        if gone > 0:
            meet(gone - 1, True)
        if gone < rounds + stages:
            meet(gone, False)
        gone += 1

    def send(ch):
        @pl.when(has_mate)
        def _():
            pick(ch)
            halo_copy(ch).start()

    advance()
    for ch in range(1, min(2, nch)):
        send(ch)
    advance()

    @pl.when(has_other)
    def _():
        ids_copy().wait_recv()
        half = hob.shape[1]
        l = lists[:, pl.ds(pl.multiple_of(odd * half, half), half)]
        hi, lo = l // 128, l % 128
        i = lax.broadcasted_iota(jnp.int32, (n_rows // 128, half), 0)
        k = lax.broadcasted_iota(jnp.int32, (128, half), 0)
        named = jnp.where(i == hi, (hob[...] + 1).astype(F), 0.0).astype(BF)
        ones = jnp.where(k == lo, 1.0, 0.0).astype(BF)
        ids = lax.dot_general(named, ones, (((1,), (1,)), ((), ())), preferred_element_type=F)
        for c in range(n_rows // 128):
            lids[:, 128 * c : 128 * c + 128] = ids[c : c + 1, :] - 1.0
        gram(G2, TR[...], rows[...], lids[...], False)
        pack_diagonals(G2, r_i, c_i)
        for k in range(pieces):
            stage_start(osums, 0, k)

    @pl.when(jnp.logical_not(has_other))
    def _():
        OG[...] = jnp.zeros_like(OG)

    advance()
    for ch in range(2, nch):
        send(ch)

    n_born = born.shape[0]
    ii = lax.broadcasted_iota(jnp.int32, (n_born, n_born), 0)
    jj = lax.broadcasted_iota(jnp.int32, (n_born, n_born), 1)
    own = jnp.broadcast_to(own_r[...].astype(F), (n_born, n_born))
    same = (own.T == own) & (ii < jj)
    rank = jnp.sum(jnp.where(same, 1.0, 0.0), axis=0, keepdims=True).astype(jnp.int32)
    base = own_r[...] * slab + rank * cols
    m = lax.broadcasted_iota(jnp.int32, (total * slab, n_born), 0)
    acc = jnp.zeros((total * slab, 128), F)
    for c in range(cols):
        oh = jnp.where(m == base + c, 1.0, 0.0).astype(BF)
        acc += jnp.dot(oh, born[:, c * 128 : (c + 1) * 128], preferred_element_type=F)
    bpack[...] = acc.astype(BF)

    @pl.when(has_other)
    def _():
        stage_through(osums, range(pieces))

    while gone <= rounds + stages:
        advance()

    def born_copy(to, frm):
        return pltpu.make_async_remote_copy(
            src_ref=bpack.at[pl.ds(pl.multiple_of(to * slab, slab), slab), :],
            dst_ref=brecv.at[pl.ds(pl.multiple_of(frm * slab, slab), slab), :],
            send_sem=bss.at[to], recv_sem=brs.at[frm],
            device_id={"dom": to // reps, "rep": to % reps}, device_id_type=mesh_id)

    def born_send(k, _):
        to = (me + k) % total
        born_copy(to, me).start()
        return 0

    lax.fori_loop(1, total, born_send, 0)
    mine = pl.ds(pl.multiple_of(me * slab, slab), slab)
    local = pltpu.make_async_copy(bpack.at[mine, :], brecv.at[mine, :], lsem)
    local.start()

    gram(G, TR[...], rows[...], eblk[...], False)

    def born_wait(k, _):
        frm = (me + k) % total
        born_copy(frm, frm).wait_recv()
        return 0

    def add_born():
        lax.fori_loop(1, total, born_wait, 0)
        local.wait()
        n = total * cap
        mm = lax.broadcasted_iota(jnp.int32, (n, total * slab), 0)
        kk = lax.broadcasted_iota(jnp.int32, (n, total * slab), 1)
        Bv = brecv[...]
        V = jnp.concatenate(
            [jnp.dot(jnp.where(kk == mm * cols + c, 1.0, 0.0).astype(BF), Bv, preferred_element_type=F)
             for c in range(cols)], axis=1)
        VT = V.T.astype(BF)
        V = V.astype(BF)
        for j in range(cols):
            o = 128 * j
            S[o:, o : o + 128] = scale * jnp.dot(VT[o:, :], V[:, o : o + 128], preferred_element_type=F)
            S[o : o + 128, o : o + 128] += jnp.where(r_i == c_i, mass[:, o : o + 128], 0.0)

    scale = 1.0 / width

    def add_halo(first, last):
        @pl.when(has_mate)
        def _():
            at = pl.ds(CH * first, CH * (last - first))
            T = rbuf[:, at]
            gram(G, T, T.T, hblk[1 - odd, :, at], True)

    def arrive(ch):
        @pl.when(has_mate)
        def _():
            halo_copy(ch).wait_recv()

    @pl.when(has_other)
    def _():
        for k in range(pieces):
            stage_finish(osums, stages - 1, k)

    for ch in range(nch - 1):
        arrive(ch)
    if nch > 1:
        add_halo(0, nch - 1)
    arrive(nch - 1)

    add_halo(nch - 1, nch)
    pack_diagonals(G, r_i, c_i)
    for k in range(pieces):
        stage_start(dsums, 0, k)
    stage_through(dsums, range(1))
    add_born()

    @pl.when(has_other)
    def _():
        for k in range(pieces):
            owner_copy(k).start()

    stage_through(dsums, range(1, pieces))

    def take(k):
        at = pl.ds(*parts[k])
        (cp, _, slot), = stage(*dsums, stages - 1, k)
        cp.wait_recv()

        @pl.when(has_other)
        def _():
            owner_copy(k).wait_recv()

        def value(first, count):
            at = pl.ds(first, count)
            return scale * (G[q, at, :] + RB[slot, at, :] + OG[at, :])

        def pair(j):
            X = value(diag[j], 128)
            XT = X.T
            ends = DG[j // 2 : j // 2 + 1, :]
            S[128 * j : 128 * j + 128, 128 * j : 128 * j + 128] += jnp.where(c_i <= r_i, X, XT)
            o = 128 * j + 128
            S[o : o + 128, o : o + 128] += jnp.where(c_i > r_i, X, jnp.where(c_i < r_i, XT, ends))

        def column(j):
            o = 128 * j
            S[o + 128 :, o : o + 128] += value(rest[j], width - o - 128)

        if k == 0:
            DG[...] = value(120, 8)
            pair(0)
        elif k % 2 == 0:
            column(k - 1)
            pair(k)
        else:
            column(k - 1)

    def take_to(last):
        nonlocal taken
        while taken <= last:
            take(taken)
            taken += 1

    def leave(j):
        at = pl.ds(128 * j, 128)
        return pltpu.make_async_copy(LO.at[:, at], out.at[:, at], fsem.at[j])

    taken = 0
    for j in range(cols - 1):
        o, m, e = 128 * j, 128 * j + 128, 128 * j + 256
        take_to(j - j % 2)
        Ld, W = chol_diag(S[o:m, o:m], A.at[j % 2])
        LO[o:m, o:m] = Ld
        if j:
            LO[:o, o:m] = jnp.zeros((o, 128), F)
        take_to(j + 1)
        near_rows = dot_t(S[m:e, o:m], W)
        S[m:e, m:e] = S[m:e, m:e] - dot_t(near_rows, near_rows)
        LO[m:e, o:m] = near_rows
        if e < width:
            far_rows = dot_t(S[e:, o:m], W)
            LO[e:, o:m] = far_rows
            S[e:, m:e] = S[e:, m:e] - dot_t(far_rows, near_rows)
            for c in range(e, width, 128):
                S[c:, c : c + 128] = S[c:, c : c + 128] - dot_t(far_rows[c - e :], far_rows[c - e : c - e + 128])
        leave(j).start()
    tail[...] = S[width - 128 :, width - 128 :]

    stages_done(dsums)

    @pl.when(has_other)
    def _():
        ids_copy().wait_send()
        stages_done(osums)
        for k in range(pieces):
            owner_copy(k).wait_send()

    def born_done(k, _):
        to = (me + k) % total
        born_copy(to, me).wait_send()
        return 0

    lax.fori_loop(1, total, born_done, 0)

    @pl.when(has_mate)
    def _():
        for ch in range(nch):
            halo_copy(ch).wait_send()


    for j in range(cols - 1):
        leave(j).wait()


def finish_kernel(L, D, out, A):
    width = out.shape[0]
    cut = width - 128
    out[:, :cut] = L[...]
    out[:cut, cut:] = jnp.zeros((cut, 128), F)
    out[cut:, cut:] = chol_diag(D[...], A, inverse=False)


def solution(mesh):
    doms, reps = mesh.shape["dom"], mesh.shape["rep"]
    total = doms * reps

    def local(elem_rows, elem_block, send_lists, halo_block, born_rows, born_owner, mass):
        n_rows, width = elem_rows.shape
        half = send_lists.shape[0] // 2
        nch = half // CH
        _, _, parts, tri = layout(width)
        pieces = len(parts)
        slab = CAP * (width // 128)
        rounds = max(1, (doms - 1).bit_length())
        stages = max(1, reps.bit_length() - 1)
        dma = pltpu.SemaphoreType.DMA
        vm = pl.BlockSpec(memory_space=pltpu.VMEM)
        far = pl.BlockSpec(memory_space=pl.ANY)
        L, D = pl.pallas_call(
            functools.partial(exchange_kernel, doms, reps, CAP),
            out_shape=(jax.ShapeDtypeStruct((width, width - 128), F), jax.ShapeDtypeStruct((128, 128), F)),
            in_specs=[vm] * 7,
            out_specs=(far, vm),
            scratch_shapes=[
                pltpu.VMEM((width, width), F),
                pltpu.VMEM((2, 128, 256), F),
                pltpu.VMEM((width, width - 128), F),
                pltpu.VMEM((8, 128), F),
                pltpu.VMEM((width, n_rows), BF),
                pltpu.VMEM((width, half), BF),
                pltpu.VMEM((width, half), BF),
                pltpu.VMEM((1, n_rows), F),
                pltpu.VMEM((1, half), jnp.int32),
                pltpu.VMEM((reps, tri, 128), F),
                pltpu.VMEM((reps - 1, tri, 128), F),
                pltpu.VMEM((reps, tri, 128), F),
                pltpu.VMEM((reps - 1, tri, 128), F),
                pltpu.VMEM((tri, 128), F),
                pltpu.VMEM((total * slab, 128), BF),
                pltpu.VMEM((total * slab, 128), BF),
                dma((nch,)),
                dma((nch,)),
                dma,
                dma,
                dma((total,)),
                dma((total,)),
                dma(((reps - 1) * pieces,)),
                dma(((reps - 1) * pieces,)),
                dma(((reps - 1) * pieces,)),
                dma(((reps - 1) * pieces,)),
                dma((pieces,)),
                dma((pieces,)),
                dma,
                pltpu.SemaphoreType.REGULAR((rounds,)),
                pltpu.SemaphoreType.REGULAR((stages,)),
                dma((width // 128 - 1,)),
            ],
            compiler_params=pltpu.CompilerParams(
                collective_id=0, has_side_effects=True, vmem_limit_bytes=63 * 1024 * 1024),
        )(elem_rows, elem_block[None, :], send_lists[None, :], halo_block.reshape(2, 1, half),
          born_rows, born_owner.reshape(1, -1), mass[None, :])
        return pl.pallas_call(
            finish_kernel,
            out_shape=jax.ShapeDtypeStruct((width, width), F),
            in_specs=[vm, vm],
            out_specs=vm,
            scratch_shapes=[pltpu.VMEM((128, 128), F)],
        )(L, D)

    both = P(("dom", "rep"))
    rows2 = P(("dom", "rep"), None)
    return jax.shard_map(local, mesh=mesh, in_specs=(rows2, both, both, both, rows2, rows2, both),
                         out_specs=rows2, check_vma=False)
```
